128 devices in a mesh: row: 8 (over x_lo, z), col: 16 (over x_hi, y, core).
Axes of the slice: x: 4 (x_hi: 2, x_lo: 2; x = x_hi * 2 + x_lo), y: 4, z: 4, core: 2. Of those that a mesh axis runs over, the one named last changes fastest.
Arguments:
- amplitudes: bfloat16 [8192, 4096], P('row', 'col'), may hold values from -6 to 6
- amp_mask: int32 [64, 32], P('row', 'col'), may hold values 0 or 1
- integrals: bfloat16 [4096, 32768], P('row', 'col'), may hold values from -0.1875 to 0.1875
- int_tiles: int32 [8, 16, 32], P(None, 'col'), may hold values from 0 to 64, as said below
- pair_dest: int32 [8192], P('row'), may hold values from 0 to 15, as said below
Outputs:
- moved: bfloat16 [16384, 32768], P(('row', 'col'))
The draws below stay inside these ranges and needn't reach their ends.
Inputs may be any that keep to these rules, and one draw needn't show every extreme that they name: `int_tiles`: entry t of a list names the nonzero tile (t // 16, t mod 16) of that integral block; the entries naming tiles are distinct, the value 64 marks an empty entry, and some block has all 32 entries filled. `pair_dest`: within each row block of 1024 consecutive pairs no column index is named by more than 128 pairs, and one is named by exactly 128.
All inputs are finite; a program needn't handle non-finite values. No bound on the sum of `amp_mask` on one device may be relied on, other than what follows from the above.
Results may differ from the reference program's by a relative error of at most 0.001.
Values may be sent and summed in bfloat16 or wider, within the bound.
A program may use at most 128 MiB of HBM per device.

```python
import jax
import jax.numpy as jnp
from jax import lax

TILE = 128
NTC = 16
GRID_ROWS = 8
GRID_COLS = 16
PAIR_DEV = 1024
PTILES = 64
P_SIZE = 8192
KT = 32
K = 4096
KRT = 4
NT = 256
N = 32768
BTILES = 64
NZMAX = 32
CAP = 128
SLOTS = 16384


def draw_int_tiles(key, part):
    blocks_all = GRID_ROWS * GRID_COLS
    count_key, full_key, order_key = jax.random.split(key, 3)
    counts = jax.random.randint(count_key, (blocks_all,), max(1, NZMAX // 4), NZMAX + 1)
    fullest = jax.random.randint(full_key, (), 0, blocks_all)
    counts = jnp.where(jnp.arange(blocks_all) == fullest, NZMAX, counts)
    order_keys = jax.random.split(order_key, blocks_all)

    def order_one(each_key):
        return jax.random.permutation(each_key, BTILES)
    orders = jax.vmap(order_one)(order_keys)
    chosen = orders[:, :NZMAX].astype(jnp.int32)
    slot_ids = jnp.arange(NZMAX)[None, :]
    listed = jnp.where(slot_ids < counts[:, None], chosen, BTILES)
    return listed.reshape(GRID_ROWS, GRID_COLS, NZMAX).astype(jnp.int32)


def draw_pair_dest(key, part):
    remaining = PAIR_DEV - CAP
    others = GRID_COLS - 1
    even_share = remaining // others
    leftover = remaining - even_share * others
    pair_count = others // 2
    busy_key, move_key, perm_key = jax.random.split(key, 3)
    busiest_all = jax.random.randint(busy_key, (GRID_ROWS,), 0, GRID_COLS)
    moves_all = jax.random.randint(move_key, (GRID_ROWS, pair_count), 0, even_share // 2 + 1)
    perm_keys = jax.random.split(perm_key, GRID_ROWS)

    def dest_row(row_key, busiest, moves):
        other_ids = jnp.arange(others)
        counts = even_share + (other_ids < leftover).astype(jnp.int32)
        transfer = jnp.zeros((others,), jnp.int32)
        transfer = transfer.at[0:2 * pair_count:2].add(moves)
        transfer = transfer.at[1:2 * pair_count:2].add(-moves)
        counts = counts + transfer
        bounds = jnp.cumsum(counts)
        positions = jnp.arange(remaining)
        chosen = jnp.sum((positions[:, None] >= bounds[None, :]).astype(jnp.int32), axis=1)
        chosen = chosen + (chosen >= busiest).astype(jnp.int32)
        labels = jnp.concatenate([jnp.full((CAP,), busiest, jnp.int32), chosen.astype(jnp.int32)])
        return jax.random.permutation(row_key, labels)
    shuffled = jax.vmap(dest_row)(perm_keys, busiest_all, moves_all)
    return shuffled.reshape(GRID_ROWS * PAIR_DEV).astype(jnp.int32)


def touch_ends(values, own_key, smallest, high):
    longest = values.shape.index(max(values.shape))
    spots = []
    for shift in (0, 1):
        where = [jax.random.randint(jax.random.fold_in(own_key, axis), (), 0, length) for axis, length in enumerate(values.shape)]
        where[longest] = (where[longest] + shift) % values.shape[longest]
        spots.append(tuple(where))
    return values.at[spots[0]].set(smallest).at[spots[1]].set(high)


def steps_of(rng, extent, pieces, low, largest):
    def one(axis_at, parts):
        draws = jax.random.uniform(jax.random.fold_in(jax.random.fold_in(rng, 6), axis_at), (parts,), jnp.float32, low / len(pieces), largest / len(pieces))
        return jnp.repeat(jnp.exp(draws), extent[axis_at] // parts).reshape((-1,) + (1,) * (len(extent) - axis_at - 1))

    factor_of = one(*pieces[0])
    for cut in pieces[1:]:
        factor_of = factor_of * one(*cut)
    return factor_of


def noise(stream_key, shape, scale, reach, pieces=(), kind=jnp.bfloat16):
    result = jax.random.normal(stream_key, shape, jnp.float32) * scale
    if len(pieces) > 0:
        result = steps_of(stream_key, shape, pieces, -0.22, 0.18) * result
    return jnp.clip(result, min=-reach, max=reach).astype(kind)


def setup_inputs(seed: int = 0) -> dict:
    arg_keys = jax.random.split(jax.random.key(seed), 6)
    return {
        "amplitudes": noise(arg_keys[0], (P_SIZE, K), 1.0, 6.0, ((0, 8), (1, 16))),
        "amp_mask": touch_ends((jax.random.randint(arg_keys[1], (PTILES, KT), 0, 2) < 1).astype(jnp.int32), jax.random.fold_in(arg_keys[1], 1), 0, 1),
        "integrals": noise(arg_keys[2], (K, N), (K // 4) ** -0.5, 0.1875, ((0, 8), (1, 16))),
        "int_tiles": draw_int_tiles(jax.random.fold_in(arg_keys[5], 71), 0),
        "pair_dest": draw_pair_dest(jax.random.fold_in(arg_keys[5], 71), 0),
    }


def tile_mask(int_tiles):
    tile_ids = jnp.arange(BTILES, dtype=jnp.int32)
    present = jnp.any(int_tiles[:, :, :, None] == tile_ids[None, None, None, :], axis=2)
    present = present.reshape(GRID_ROWS, GRID_COLS, KRT, NTC).transpose(0, 2, 1, 3)
    return present.reshape(KT, NT)


def reference(amplitudes, amp_mask, integrals, int_tiles, pair_dest):
    amp_scale = amp_mask.astype(jnp.bfloat16)
    amp_used = (amplitudes.reshape(PTILES, TILE, KT, TILE) * amp_scale[:, None, :, None]).reshape(P_SIZE, K)
    int_scale = tile_mask(int_tiles).astype(jnp.bfloat16)
    int_used = (integrals.reshape(KT, TILE, NT, TILE) * int_scale[:, None, :, None]).reshape(K, N)

    def one_block(block_pair):
        pair_rows, targets = block_pair
        ladder = jnp.dot(pair_rows, int_used, preferred_element_type=jnp.float32).astype(jnp.bfloat16)
        col_ids = jnp.arange(GRID_COLS, dtype=jnp.int32)
        onehot = (targets[:, None] == col_ids[None, :]).astype(jnp.int32)
        before = jnp.cumsum(onehot, axis=0) - onehot
        slot_of = jnp.sum(before * onehot, axis=1)
        row_place = (targets * CAP + slot_of).astype(jnp.int32)
        return jnp.zeros((GRID_COLS * CAP, N), jnp.bfloat16).at[row_place].set(ladder)

    moved = lax.map(one_block, (amp_used.reshape(GRID_ROWS, PAIR_DEV, K), pair_dest.reshape(GRID_ROWS, PAIR_DEV)))
    return moved.reshape(SLOTS, N)
```

```python
import functools

import jax
import jax.numpy as jnp
from jax import lax
from jax.experimental import pallas as pl
from jax.experimental.pallas import tpu as pltpu
from jax.sharding import PartitionSpec as P

TILE = 128
MESH = pl.DeviceIdType.MESH
CAP = 128
CHUNK_TILES = 2
CHUNK = CHUNK_TILES * TILE
GROUPS = (16, 8, 8)


def ladder_kernel(
    send_tiles, positions, amp_scale, pair_dest, amp_hbm, int_hbm, out,
    amp_in, int_in, panel, comp, dense, select, key, lad, stage,
    load_sem, amp_send, amp_recv, int_send, int_recv, out_send, out_recv, own_sem,
):
    row, col = lax.axis_index("row"), lax.axis_index("col")
    n_cols = lax.axis_size("col")
    n_rows = lax.axis_size("row")
    pair_rows, amp_cols = amp_hbm.shape
    k_tiles, _, int_cols = int_hbm.shape
    n_tiles = int_cols // TILE
    n_chunks = n_tiles // CHUNK_TILES
    half_rows = pair_rows // 2

    core, y, x_hi = lax.rem(col, 2), lax.rem(lax.div(col, 2), 4), lax.div(col, 8)
    z, x_lo = lax.rem(row, 4), lax.div(row, 4)

    def col_at(dx, dy, dc):
        return lax.rem(x_hi + dx, 2) * 8 + lax.rem(y + dy + 4, 4) * 2 + lax.rem(core + dc, 2)

    def row_at(dx, dz):
        return lax.rem(x_lo + dx, 2) * 4 + lax.rem(z + dz + 4, 4)

    load_amp = pltpu.make_async_copy(amp_hbm, amp_in, load_sem.at[0])
    load_amp.start()
    load_ints = [
        pltpu.make_async_copy(
            int_hbm.at[:, :, n * TILE:(n + 1) * TILE], int_in.at[n * k_tiles:(n + 1) * k_tiles], load_sem.at[1 + n]
        )
        for n in range(n_tiles)
    ]
    for load in load_ints:
        load.start()

    barrier = pltpu.get_barrier_semaphore()
    for step in range(1, n_cols):
        peer = lax.rem(col + step, n_cols)
        pl.semaphore_signal(barrier, inc=1, device_id=(row, peer), device_id_type=MESH)
    for dx, dz in ((1, 0), (0, 1), (0, -1)):
        pl.semaphore_signal(barrier, inc=1, device_id=(row_at(dx, dz), col), device_id_type=MESH)

    load_amp.wait()
    own_cols = pl.ds(pl.multiple_of(col * amp_cols, amp_cols), amp_cols)
    for a in range(pair_rows // TILE):
        rows = slice(a * TILE, (a + 1) * TILE)
        panel[rows, own_cols] = amp_in[rows, :] * amp_scale[a:a + 1, :]

    for load in load_ints:
        load.wait()
    first = 0
    for g, count in enumerate(GROUPS):
        for slot in range(count):
            comp[g][row * count + slot] = int_in[send_tiles[first + slot]]
        comp[g][n_rows * count] = jnp.zeros((TILE, TILE), jnp.bfloat16)
        first += count

    pl.semaphore_wait(barrier, n_cols - 1 + 3)

    def amp_piece(owner, half):
        at = pl.ds(pl.multiple_of(owner * amp_cols, amp_cols), amp_cols)
        if half is None:
            return panel.at[:, at]
        return panel.at[half * half_rows:(half + 1) * half_rows, at]

    def amp_copy(sem, owner, half, target):
        piece = amp_piece(owner, half)
        return pltpu.make_async_remote_copy(
            piece, piece, amp_send.at[sem], amp_recv.at[sem], device_id=(row, target), device_id_type=MESH
        )

    def int_piece(g, owner, half):
        count = GROUPS[g]
        if half is None:
            return comp[g].at[pl.ds(owner * count, count)]
        return comp[g].at[pl.ds(owner * count + half * (count // 2), count // 2)]

    def int_copy(sem, g, owner, half, target):
        piece = int_piece(g, owner, half)
        return pltpu.make_async_remote_copy(
            piece, piece, int_send.at[g, sem], int_recv.at[g, sem], device_id=(target, col), device_id_type=MESH
        )

    amp_steps = {
        0: ((0, 0, 0), None, (1, 0, 0), (1, 0, 0)),
        1: ((0, 0, 0), None, (0, 1, 0), (0, -1, 0)),
        2: ((0, 0, 0), None, (0, -1, 0), (0, 1, 0)),
        3: ((1, 0, 0), None, (0, 1, 0), (1, -1, 0)),
        4: ((1, 0, 0), None, (0, -1, 0), (1, 1, 0)),
        5: ((0, -1, 0), 0, (0, 1, 0), (0, 2, 0)),
        6: ((0, 1, 0), 1, (0, -1, 0), (0, 2, 0)),
        7: ((1, -1, 0), 0, (0, 1, 0), (1, 2, 0)),
        8: ((1, 1, 0), 1, (0, -1, 0), (1, 2, 0)),
        9: ((0, 0, 0), None, (0, 0, 1), (0, 0, 1)),
        10: ((0, -1, 0), None, (0, 0, 1), (0, -1, 1)),
        11: ((0, 1, 0), None, (0, 0, 1), (0, 1, 1)),
        12: ((1, 0, 0), None, (0, 0, 1), (1, 0, 1)),
        13: ((1, -1, 0), None, (0, 0, 1), (1, -1, 1)),
        14: ((1, 1, 0), None, (0, 0, 1), (1, 1, 1)),
        15: ((0, 2, 0), None, (0, 0, 1), (0, 2, 1)),
        16: ((1, 2, 0), None, (0, 0, 1), (1, 2, 1)),
    }
    int_steps = {
        0: ((0, 0), None, (1, 0), (1, 0)),
        1: ((0, 0), None, (0, 1), (0, -1)),
        2: ((0, 0), None, (0, -1), (0, 1)),
        3: ((1, 0), None, (0, 1), (1, -1)),
        4: ((1, 0), None, (0, -1), (1, 1)),
        5: ((0, -1), 0, (0, 1), (0, 2)),
        6: ((0, 1), 1, (0, -1), (0, 2)),
        7: ((1, -1), 0, (0, 1), (1, 2)),
        8: ((1, 1), 1, (0, -1), (1, 2)),
    }

    def amp_start(*sems):
        for sem in sems:
            what, half, to, _ = amp_steps[sem]
            amp_copy(sem, col_at(*what), half, col_at(*to)).start()

    def amp_arrived(*sems):
        for sem in sems:
            _, half, to, comes = amp_steps[sem]
            amp_copy(sem, col_at(*comes), half, col_at(*to)).wait_recv()

    def int_start(g, *sems):
        for sem in sems:
            what, half, to, _ = int_steps[sem]
            int_copy(sem, g, row_at(*what), half, row_at(*to)).start()

    def int_arrived(g, *sems):
        for sem in sems:
            _, half, to, comes = int_steps[sem]
            int_copy(sem, g, row_at(*comes), half, row_at(*to)).wait_recv()

    amp_start(0, 1, 2, 9)
    int_start(0, 1, 2, 0)
    for g in range(1, len(GROUPS)):
        int_start(g, 0)

    for block in range(pair_rows // TILE):
        cols = slice(block * TILE, (block + 1) * TILE)
        q = lax.broadcasted_iota(jnp.int32, (pair_rows, TILE), 0)
        p = lax.broadcasted_iota(jnp.int32, (pair_rows, TILE), 1) + block * TILE
        earlier = jnp.where(q < p, 1.0, 0.0).astype(jnp.bfloat16)
        dest_all = lax.broadcasted_iota(jnp.int32, (n_cols, pair_rows), 0)
        onehot = jnp.where(dest_all == pair_dest[...], 1.0, 0.0)
        before = jnp.dot(onehot.astype(jnp.bfloat16), earlier, preferred_element_type=jnp.float32)
        slot = jnp.sum(before * onehot[:, cols], axis=0, keepdims=True)
        key[:, cols] = pair_dest[:, cols] * CAP + slot.astype(jnp.int32)

    def fill_select(d, carry):
        places = lax.broadcasted_iota(jnp.int32, (CAP, pair_rows), 0) + d * CAP
        at = pl.ds(pl.multiple_of(d * CAP, CAP), CAP)
        select[at, :] = jnp.where(places == key[...], 1.0, 0.0).astype(jnp.bfloat16)
        return carry

    lax.fori_loop(0, n_cols, fill_select, 0)

    amp_arrived(1, 2)
    amp_start(5, 6, 10, 11)
    int_arrived(0, 1, 2)
    int_start(0, 5, 6)
    amp_arrived(0)
    amp_start(3, 4, 12)
    int_arrived(0, 0)
    int_start(0, 3, 4)
    amp_arrived(5, 6)
    amp_start(15)
    int_arrived(0, 5, 6)
    amp_arrived(3, 4)
    amp_start(7, 8, 13, 14)
    int_arrived(0, 3, 4)
    int_start(0, 7, 8)
    int_start(1, 1, 2)
    int_arrived(1, 0)
    int_start(1, 3, 4)
    amp_arrived(7, 8)
    amp_start(16)
    amp_arrived(9, 10, 11, 12, 13, 14, 15, 16)
    int_arrived(0, 7, 8)

    def unpack(q, groups):
        def one_row(r, carry):
            for n in range(CHUNK_TILES):
                for k in range(k_tiles):
                    tile = None
                    for g in range(groups):
                        at = positions[((g * n_rows + r) * n_tiles + q * CHUNK_TILES + n) * k_tiles + k]
                        part = comp[g][at]
                        tile = part if tile is None else tile + part
                    down = pl.ds(pl.multiple_of((r * k_tiles + k) * TILE, TILE), TILE)
                    dense[down, n * TILE:(n + 1) * TILE] = tile
            return carry

        lax.fori_loop(0, n_rows, one_row, 0)

    def multiply(q):
        m_rows = pair_rows // 2

        def one_half(m, carry):
            at = pl.ds(pl.multiple_of(m * m_rows, m_rows), m_rows)
            lad[at, :] = jnp.dot(panel[at, :], dense[...], preferred_element_type=jnp.float32).astype(jnp.bfloat16)
            return carry

        lax.fori_loop(0, 2, one_half, 0)
        dests = 4

        def one_part(j, carry):
            at = pl.ds(pl.multiple_of(j * dests * CAP, dests * CAP), dests * CAP)
            rows = jnp.dot(select[at, :], lad[...], preferred_element_type=jnp.float32).astype(jnp.bfloat16)
            stage[q, pl.ds(j * dests, dests)] = rows.reshape(dests, CAP, CHUNK)
            return carry

        lax.fori_loop(0, n_cols // dests, one_part, 0)

    def out_piece(owner, q):
        return out.at[:, pl.ds(pl.multiple_of(owner * int_cols + q * CHUNK, CHUNK), CHUNK)]

    def send(q):
        def one_peer(step, carry):
            peer = lax.rem(col + step, n_cols)
            pltpu.make_async_remote_copy(
                stage.at[q, peer], out_piece(col, q), out_send.at[step], out_recv.at[step],
                device_id=(row, peer), device_id_type=MESH,
            ).start()
            return carry

        lax.fori_loop(1, n_cols, one_peer, 0)
        pltpu.make_async_copy(stage.at[q, col], out_piece(col, q), own_sem.at[q]).start()

    def chunks(lo, hi, groups):
        def one_chunk(q, carry):
            unpack(q, groups)
            multiply(q)
            send(q)
            return carry

        lax.fori_loop(lo, hi, one_chunk, 0)

    chunks(0, 2, 1)
    int_arrived(1, 1, 2)
    int_start(1, 5, 6)
    int_arrived(1, 3, 4)
    int_start(1, 7, 8)
    int_start(2, 1, 2)
    int_arrived(2, 0)
    int_start(2, 3, 4)
    int_arrived(1, 5, 6, 7, 8)
    chunks(2, 3, 2)
    int_arrived(2, 1, 2)
    int_start(2, 5, 6)
    int_arrived(2, 3, 4)
    int_start(2, 7, 8)
    int_arrived(2, 5, 6, 7, 8)
    chunks(3, n_chunks, 3)

    for sem in amp_steps:
        what, half, to, _ = amp_steps[sem]
        amp_copy(sem, col_at(*what), half, col_at(*to)).wait_send()
    for g in range(len(GROUPS)):
        for sem in int_steps:
            what, half, to, _ = int_steps[sem]
            int_copy(sem, g, row_at(*what), half, row_at(*to)).wait_send()

    def own_done(q, carry):
        pltpu.make_async_copy(stage.at[q, col], out_piece(col, q), own_sem.at[q]).wait()
        return carry

    lax.fori_loop(0, n_chunks, own_done, 0)

    def peer_done(step, carry):
        source = lax.rem(col - step + n_cols, n_cols)
        block = out.at[:, pl.ds(pl.multiple_of(source * int_cols, int_cols), int_cols)]
        whole = pltpu.make_async_remote_copy(
            block, block, out_send.at[step], out_recv.at[step], device_id=(row, source), device_id_type=MESH
        )
        whole.wait()
        return carry

    lax.fori_loop(1, n_cols, peer_done, 0)


def copy_kernel(src, dst, buf, in_sem, out_sem):
    parts = buf.shape[0]
    width = src.shape[1] // parts
    reads = [
        pltpu.make_async_copy(src.at[:, i * width:(i + 1) * width], buf.at[i], in_sem.at[i]) for i in range(parts)
    ]
    writes = [
        pltpu.make_async_copy(buf.at[i], dst.at[:, i * width:(i + 1) * width], out_sem.at[i]) for i in range(parts)
    ]
    for read in reads:
        read.start()
    for read, write in zip(reads, writes):
        read.wait()
        write.start()
    for write in writes:
        write.wait()


def on_device(amplitudes, amp_mask, integrals, int_tiles, pair_dest):
    pair_rows, amp_cols = amplitudes.shape
    int_rows, int_cols = integrals.shape
    n_rows, n_cols = lax.axis_size("row"), lax.axis_size("col")
    k_tiles, n_tiles = int_rows // TILE, int_cols // TILE
    block_tiles = k_tiles * n_tiles
    slots = int_tiles.shape[2]
    n_chunks = n_tiles // CHUNK_TILES

    ids = jnp.arange(block_tiles, dtype=jnp.int32)
    tile_of = (ids % k_tiles) * n_tiles + ids // k_tiles
    present = jnp.any(int_tiles[:, 0, :, None] == tile_of[None, None, :], axis=1)
    ahead = present[:, :, None] & (ids[:, None] < ids[None, :])[None]
    rank = jnp.sum(ahead.astype(jnp.int32), axis=1)
    parts, first = [], 0
    for count in GROUPS:
        inside = present & (rank >= first) & (rank < first + count)
        place = jnp.arange(n_rows, dtype=jnp.int32)[:, None] * count + rank - first
        parts.append(jnp.where(inside, place, n_rows * count))
        first += count
    positions = jnp.stack(parts).reshape(-1)
    me = lax.axis_index("row")
    own_present = lax.dynamic_index_in_dim(present, me, 0, keepdims=False)
    own_rank = lax.dynamic_index_in_dim(rank, me, 0, keepdims=False)
    hit = own_present[None, :] & (own_rank[None, :] == jnp.arange(slots, dtype=jnp.int32)[:, None])
    send_tiles = jnp.sum(jnp.where(hit, ids[None, :], 0), axis=1)
    amp_scale = jnp.repeat(amp_mask.astype(jnp.bfloat16), TILE, axis=1)

    any_ref = pl.BlockSpec(memory_space=pl.ANY)
    smem = pl.BlockSpec(memory_space=pltpu.SMEM)
    vmem = pl.BlockSpec(memory_space=pltpu.VMEM)
    spread = pl.pallas_call(
        ladder_kernel,
        out_shape=jax.ShapeDtypeStruct((CAP, n_cols * int_cols), jnp.bfloat16),
        in_specs=[smem, smem, vmem, vmem, any_ref, any_ref],
        out_specs=any_ref,
        scratch_shapes=[
            pltpu.VMEM((pair_rows, amp_cols), jnp.bfloat16),
            pltpu.VMEM((block_tiles, TILE, TILE), jnp.bfloat16),
            pltpu.VMEM((pair_rows, n_cols * amp_cols), jnp.bfloat16),
            [pltpu.VMEM((n_rows * count + 1, TILE, TILE), jnp.bfloat16) for count in GROUPS],
            pltpu.VMEM((n_rows * int_rows, CHUNK), jnp.bfloat16),
            pltpu.VMEM((n_cols * CAP, pair_rows), jnp.bfloat16),
            pltpu.VMEM((1, pair_rows), jnp.int32),
            pltpu.VMEM((pair_rows, CHUNK), jnp.bfloat16),
            pltpu.VMEM((n_chunks, n_cols, CAP, CHUNK), jnp.bfloat16),
            pltpu.SemaphoreType.DMA((1 + n_tiles,)),
            pltpu.SemaphoreType.DMA((17,)),
            pltpu.SemaphoreType.DMA((17,)),
            pltpu.SemaphoreType.DMA((len(GROUPS), 9)),
            pltpu.SemaphoreType.DMA((len(GROUPS), 9)),
            pltpu.SemaphoreType.DMA((n_cols,)),
            pltpu.SemaphoreType.DMA((n_cols,)),
            pltpu.SemaphoreType.DMA((n_chunks,)),
        ],
        name="ladder",
        compiler_params=pltpu.CompilerParams(
            collective_id=0, has_side_effects=True, vmem_limit_bytes=56 * 1024 * 1024
        ),
    )(
        send_tiles, positions, amp_scale, pair_dest.reshape(1, pair_rows), amplitudes,
        integrals.reshape(k_tiles, TILE, int_cols),
    )
    parts_out = 8
    return pl.pallas_call(
        copy_kernel,
        out_shape=jax.ShapeDtypeStruct(spread.shape, spread.dtype),
        in_specs=[any_ref],
        out_specs=any_ref,
        scratch_shapes=[
            pltpu.VMEM((parts_out, CAP, n_cols * int_cols // parts_out), jnp.bfloat16),
            pltpu.SemaphoreType.DMA((parts_out,)),
            pltpu.SemaphoreType.DMA((parts_out,)),
        ],
        name="deliver",
    )(spread)


def solution(mesh):
    in_specs = (P("row", "col"), P("row", "col"), P("row", "col"), P(None, "col", None), P("row"))
    out_specs = P(("row", "col"), None)
    return jax.shard_map(
        on_device, mesh=mesh, in_specs=in_specs, out_specs=out_specs, check_vma=False
    )
```

```python
import functools

import jax
import jax.numpy as jnp
from jax import lax
from jax.experimental import pallas as pl
from jax.experimental.pallas import tpu as pltpu
from jax.sharding import PartitionSpec as P

TILE = 128
MESH = pl.DeviceIdType.MESH
CAP = 128
CHUNK_TILES = 2
CHUNK = CHUNK_TILES * TILE
GROUPS = (8, 8, 8, 8)
PART = 4

AMP_STEPS = {
    "x0": ((0, 0, 0), 0, (1, 0, 0)),
    "x1": ((0, 0, 0), 1, (1, 0, 0)),
    "p0": ((0, 0, 0), 0, (0, 1, 0)),
    "p1": ((0, 0, 0), 1, (0, 1, 0)),
    "m0": ((0, 0, 0), 0, (0, -1, 0)),
    "m1": ((0, 0, 0), 1, (0, -1, 0)),
    "pp": ((0, -1, 0), 0, (0, 1, 0)),
    "mm": ((0, 1, 0), 1, (0, -1, 0)),
    "xp0": ((1, 0, 0), 0, (0, 1, 0)),
    "xp1": ((1, 0, 0), 1, (0, 1, 0)),
    "xm0": ((1, 0, 0), 0, (0, -1, 0)),
    "xm1": ((1, 0, 0), 1, (0, -1, 0)),
    "xpp": ((1, -1, 0), 0, (0, 1, 0)),
    "xmm": ((1, 1, 0), 1, (0, -1, 0)),
    "c": ((0, 0, 0), None, (0, 0, 1)),
    "cp": ((0, -1, 0), None, (0, 0, 1)),
    "cm": ((0, 1, 0), None, (0, 0, 1)),
    "cq0": ((0, 2, 0), 0, (0, 0, 1)),
    "cq1": ((0, 2, 0), 1, (0, 0, 1)),
    "cx": ((1, 0, 0), None, (0, 0, 1)),
    "cxp": ((1, -1, 0), None, (0, 0, 1)),
    "cxm": ((1, 1, 0), None, (0, 0, 1)),
    "cxq0": ((1, 2, 0), 0, (0, 0, 1)),
    "cxq1": ((1, 2, 0), 1, (0, 0, 1)),
}
INT_STEPS = {
    "x": ((0, 0), None, (1, 0)),
    "p": ((0, 0), None, (0, 1)),
    "m": ((0, 0), None, (0, -1)),
    "pp": ((0, -1), 0, (0, 1)),
    "mm": ((0, 1), 1, (0, -1)),
    "xp": ((1, 0), None, (0, 1)),
    "xm": ((1, 0), None, (0, -1)),
    "xpp": ((1, -1), 0, (0, 1)),
    "xmm": ((1, 1), 1, (0, -1)),
}


def ladder_kernel(
    send_tiles, positions, amp_mask, pair_dest, amp_hbm, int_hbm, out,
    amp_in, int_in, panel, comp, dense, select, key, acc, lad, stage,
    load_sem, amp_send, amp_recv, int_send, int_recv, out_send, out_recv, own_sem,
):
    row, col = lax.axis_index("row"), lax.axis_index("col")
    n_cols = lax.axis_size("col")
    n_rows = lax.axis_size("row")
    pair_rows, amp_cols = amp_hbm.shape
    k_tiles, _, int_cols = int_hbm.shape
    n_tiles = int_cols // TILE
    n_chunks = n_tiles // CHUNK_TILES
    half_rows = pair_rows // 2

    core, y, x_hi = lax.rem(col, 2), lax.rem(lax.div(col, 2), 4), lax.div(col, 8)
    z, x_lo = lax.rem(row, 4), lax.div(row, 4)

    def col_at(dx, dy, dc):
        return lax.rem(x_hi + dx + 2, 2) * 8 + lax.rem(y + dy + 4, 4) * 2 + lax.rem(core + dc + 2, 2)

    def row_at(dx, dz):
        return lax.rem(x_lo + dx + 2, 2) * 4 + lax.rem(z + dz + 4, 4)

    load_amp = pltpu.make_async_copy(amp_hbm, amp_in, load_sem.at[0])
    load_amp.start()
    load_ints = [
        pltpu.make_async_copy(
            int_hbm.at[:, :, n * TILE:(n + 1) * TILE], int_in.at[n * k_tiles:(n + 1) * k_tiles], load_sem.at[1 + n]
        )
        for n in range(n_tiles)
    ]
    for load in load_ints:
        load.start()

    barrier = pltpu.get_barrier_semaphore()
    for step in range(1, n_cols):
        peer = lax.rem(col + step, n_cols)
        pl.semaphore_signal(barrier, inc=1, device_id=(row, peer), device_id_type=MESH)
    for dx, dz in ((1, 0), (0, 1), (0, -1)):
        pl.semaphore_signal(barrier, inc=1, device_id=(row_at(dx, dz), col), device_id_type=MESH)

    def amp_copy(name, seen_by_receiver):
        what, half, to = AMP_STEPS[name]
        sem = list(AMP_STEPS).index(name)
        owner = col_at(*(w - t for w, t in zip(what, to))) if seen_by_receiver else col_at(*what)
        at = pl.ds(pl.multiple_of(owner * amp_cols, amp_cols), amp_cols)
        piece = panel.at[:, at] if half is None else panel.at[half * half_rows:(half + 1) * half_rows, at]
        return pltpu.make_async_remote_copy(
            piece, piece, amp_send.at[sem], amp_recv.at[sem], device_id=(row, col_at(*to)), device_id_type=MESH
        )

    def int_copy(g, name, seen_by_receiver):
        what, half, to = INT_STEPS[name]
        sem = list(INT_STEPS).index(name)
        owner = row_at(*(w - t for w, t in zip(what, to))) if seen_by_receiver else row_at(*what)
        count = GROUPS[g]
        if half is None:
            piece = comp[g].at[pl.ds(owner * count, count)]
        else:
            piece = comp[g].at[pl.ds(owner * count + half * (count // 2), count // 2)]
        return pltpu.make_async_remote_copy(
            piece, piece, int_send.at[g, sem], int_recv.at[g, sem], device_id=(row_at(*to), col), device_id_type=MESH
        )

    def amp_start(*names):
        for name in names:
            amp_copy(name, False).start()

    def amp_arrived(*names):
        for name in names:
            amp_copy(name, True).wait_recv()

    def int_start(g, *names):
        for name in names:
            int_copy(g, name, False).start()

    def int_arrived(g, *names):
        for name in names:
            int_copy(g, name, True).wait_recv()

    load_amp.wait()
    own_cols = pl.multiple_of(col * amp_cols, amp_cols)
    kept = amp_mask[...].astype(jnp.float32).astype(jnp.bfloat16)
    for a in range(pair_rows // TILE):
        for k in range(amp_cols // TILE):
            tile = amp_in[a * TILE:(a + 1) * TILE, k * TILE:(k + 1) * TILE]
            panel[a * TILE:(a + 1) * TILE, pl.ds(own_cols + k * TILE, TILE)] = tile * kept[a:a + 1, k:k + 1]
    pl.semaphore_wait(barrier, n_cols - 1 + 3)
    amp_start("x0", "p0", "m1", "x1", "p1", "m0", "c")

    for load in load_ints:
        load.wait()
    first = 0
    for g, count in enumerate(GROUPS):
        for slot in range(count):
            comp[g][row * count + slot] = int_in[send_tiles[first + slot]]
        comp[g][n_rows * count] = jnp.zeros((TILE, TILE), jnp.bfloat16)
        first += count
    int_start(0, "x", "p", "m")
    int_start(1, "p", "m")

    dest_all = lax.broadcasted_iota(jnp.int32, (n_cols, pair_rows), 0)
    onehot = jnp.where(dest_all == pair_dest[...], 1.0, 0.0)
    for block in range(pair_rows // TILE):
        cols = slice(block * TILE, (block + 1) * TILE)
        q = lax.broadcasted_iota(jnp.int32, (pair_rows, TILE), 0)
        p = lax.broadcasted_iota(jnp.int32, (pair_rows, TILE), 1) + block * TILE
        earlier = jnp.where(q < p, 1.0, 0.0).astype(jnp.bfloat16)
        before = jnp.dot(onehot.astype(jnp.bfloat16), earlier, preferred_element_type=jnp.float32)
        slot = jnp.sum(before * onehot[:, cols], axis=0, keepdims=True)
        ahead = pair_dest[:, cols] - col
        key[:, cols] = jnp.where(ahead < 0, ahead + n_cols, ahead) * CAP + slot.astype(jnp.int32)

    def fill_select(d, carry):
        places = lax.broadcasted_iota(jnp.int32, (CAP, pair_rows), 0) + d * CAP
        at = pl.ds(pl.multiple_of(d * CAP, CAP), CAP)
        select[at, :] = jnp.where(places == key[...], 1.0, 0.0).astype(jnp.bfloat16)
        return carry

    lax.fori_loop(0, n_cols, fill_select, 0)

    def unpack(q, groups):
        def one_row(r, carry):
            for n in range(CHUNK_TILES):
                for k in range(k_tiles):
                    tile = None
                    for g in range(groups):
                        at = positions[((g * n_rows + r) * n_tiles + q * CHUNK_TILES + n) * k_tiles + k]
                        part = comp[g][at]
                        tile = part if tile is None else tile + part
                    down = pl.ds(pl.multiple_of((r * k_tiles + k) * TILE, TILE), TILE)
                    dense[down, n * TILE:(n + 1) * TILE] = tile
            return carry

        lax.fori_loop(0, n_rows, one_row, 0)

    def multiply(start, depth, first, last):
        m_rows = pair_rows // 2

        def one_half(m, carry):
            at = pl.ds(pl.multiple_of(m * m_rows, m_rows), m_rows)
            deep = pl.ds(pl.multiple_of(start, 512), depth)
            total = jnp.dot(panel[at, deep], dense[deep, :], preferred_element_type=jnp.float32)
            if not first:
                total = total + acc[at, :]
            if last:
                lad[at, :] = total.astype(jnp.bfloat16)
            else:
                acc[at, :] = total
            return carry

        lax.fori_loop(0, 2, one_half, 0)

    def out_piece(owner, q):
        return out.at[:, pl.ds(pl.multiple_of(owner * int_cols + q * CHUNK, CHUNK), CHUNK)]

    def send_part(q, j):
        for i in range(PART):
            step = j * PART + i
            peer = lax.rem(col + step, n_cols)

            def to_peer():
                pltpu.make_async_remote_copy(
                    stage.at[q, step], out_piece(col, q), out_send.at[step], out_recv.at[step],
                    device_id=(row, peer), device_id_type=MESH,
                ).start()

            if step == 0:
                pltpu.make_async_copy(stage.at[q, 0], out_piece(col, q), own_sem.at[q]).start()
            else:
                to_peer()

    n_parts = n_cols // PART

    def spread(q):
        for j in range(n_parts):
            at = slice(j * PART * CAP, (j + 1) * PART * CAP)
            rows = jnp.dot(select[at, :], lad[...], preferred_element_type=jnp.float32).astype(jnp.bfloat16)
            stage[q, j * PART:(j + 1) * PART] = rows.reshape(PART, CAP, CHUNK)
            if j > 0:
                send_part(q, j - 1)

    def chunks(lo, hi, groups):
        def one_chunk(q, carry):
            unpack(q, groups)
            send_part(q - 1, n_parts - 1)
            multiply(0, n_cols * amp_cols, True, True)
            spread(q)
            return carry

        lax.fori_loop(lo, hi, one_chunk, 0)

    amp_arrived("p0", "m1")
    amp_start("pp", "mm")
    int_arrived(0, "p", "m")
    int_start(0, "pp", "mm")
    amp_arrived("x0", "x1")
    amp_start("xp0", "xm1", "xp1", "xm0", "cx")
    int_start(1, "x")
    amp_arrived("p1", "m0")
    amp_start("cp", "cm")
    int_arrived(1, "p", "m")
    int_start(1, "pp", "mm")
    amp_arrived("pp", "mm")
    amp_start("cq0", "cq1")
    int_arrived(0, "x")
    int_start(0, "xp", "xm")
    int_start(2, "x")
    amp_arrived("xp0", "xm1")
    amp_start("xpp", "xmm")
    int_arrived(0, "xp", "xm")
    int_start(0, "xpp", "xmm")
    int_start(3, "x")
    int_arrived(1, "x")
    int_start(1, "xp", "xm")
    int_start(2, "p", "m")
    amp_arrived("c", "cp", "cm", "cq0", "cq1")
    amp_arrived("xp1", "xm0")
    amp_start("cxp", "cxm")
    int_arrived(0, "pp", "mm", "xpp", "xmm")

    y_cols = 2 * amp_cols
    x_cols = 4 * y_cols
    far = lax.rem(x_hi + 1, 2) * x_cols
    unpack(0, 1)
    multiply(x_hi * x_cols, x_cols, True, False)
    amp_arrived("cx")
    multiply(far + y * y_cols, y_cols, False, False)
    amp_arrived("xpp")
    amp_start("cxq0")
    amp_arrived("xmm")
    amp_start("cxq1")
    int_arrived(1, "xp", "xm")
    int_start(1, "xpp", "xmm")
    amp_arrived("cxp")
    multiply(far + lax.rem(y + 3, 4) * y_cols, y_cols, False, False)
    amp_arrived("cxm")
    multiply(far + lax.rem(y + 1, 4) * y_cols, y_cols, False, False)
    amp_arrived("cxq0", "cxq1")
    multiply(far + lax.rem(y + 2, 4) * y_cols, y_cols, False, True)
    spread(0)

    int_arrived(2, "x")
    int_start(2, "xp", "xm")
    int_arrived(2, "p", "m")
    int_start(2, "pp", "mm")
    int_start(3, "p", "m")
    int_arrived(1, "pp", "mm", "xpp", "xmm")
    chunks(1, 2, 2)
    int_arrived(2, "xp", "xm")
    int_start(2, "xpp", "xmm")
    int_arrived(3, "x")
    int_start(3, "xp", "xm")
    int_arrived(3, "p", "m")
    int_start(3, "pp", "mm")
    int_arrived(2, "pp", "mm", "xpp", "xmm")
    chunks(2, 3, 3)
    int_arrived(3, "xp", "xm")
    int_start(3, "xpp", "xmm")
    int_arrived(3, "pp", "mm", "xpp", "xmm")
    chunks(3, n_chunks, 4)

    for name in AMP_STEPS:
        amp_copy(name, False).wait_send()
    send_part(n_chunks - 1, n_parts - 1)
    for g in range(len(GROUPS)):
        for name in INT_STEPS:
            int_copy(g, name, False).wait_send()

    def own_done(q, carry):
        pltpu.make_async_copy(stage.at[q, 0], out_piece(col, q), own_sem.at[q]).wait()
        return carry

    lax.fori_loop(0, n_chunks, own_done, 0)

    def peer_done(step, carry):
        source = lax.rem(col - step + n_cols, n_cols)
        block = out.at[:, pl.ds(pl.multiple_of(source * int_cols, int_cols), int_cols)]
        whole = pltpu.make_async_remote_copy(
            block, block, out_send.at[step], out_recv.at[step], device_id=(row, source), device_id_type=MESH
        )
        whole.wait()
        return carry

    lax.fori_loop(1, n_cols, peer_done, 0)


def copy_kernel(src, dst, buf, in_sem, out_sem):
    parts = buf.shape[0]
    width = src.shape[1] // parts
    reads = [
        pltpu.make_async_copy(src.at[:, i * width:(i + 1) * width], buf.at[i], in_sem.at[i]) for i in range(parts)
    ]
    writes = [
        pltpu.make_async_copy(buf.at[i], dst.at[:, i * width:(i + 1) * width], out_sem.at[i]) for i in range(parts)
    ]
    for read in reads:
        read.start()
    for read, write in zip(reads, writes):
        read.wait()
        write.start()
    for write in writes:
        write.wait()


def on_device(amplitudes, amp_mask, integrals, int_tiles, pair_dest):
    pair_rows, amp_cols = amplitudes.shape
    int_rows, int_cols = integrals.shape
    n_rows, n_cols = lax.axis_size("row"), lax.axis_size("col")
    k_tiles, n_tiles = int_rows // TILE, int_cols // TILE
    block_tiles = k_tiles * n_tiles
    slots = int_tiles.shape[2]
    n_chunks = n_tiles // CHUNK_TILES

    ids = jnp.arange(block_tiles, dtype=jnp.int32)
    tile_of = (ids % k_tiles) * n_tiles + ids // k_tiles
    present = jnp.any(int_tiles[:, 0, :, None] == tile_of[None, None, :], axis=1)
    ahead = present[:, :, None] & (ids[:, None] < ids[None, :])[None]
    rank = jnp.sum(ahead.astype(jnp.int32), axis=1)
    parts, first = [], 0
    for count in GROUPS:
        inside = present & (rank >= first) & (rank < first + count)
        place = jnp.arange(n_rows, dtype=jnp.int32)[:, None] * count + rank - first
        parts.append(jnp.where(inside, place, n_rows * count))
        first += count
    positions = jnp.stack(parts).reshape(-1)
    me = lax.axis_index("row")
    own_present = lax.dynamic_index_in_dim(present, me, 0, keepdims=False)
    own_rank = lax.dynamic_index_in_dim(rank, me, 0, keepdims=False)
    hit = own_present[None, :] & (own_rank[None, :] == jnp.arange(slots, dtype=jnp.int32)[:, None])
    send_tiles = jnp.sum(jnp.where(hit, ids[None, :], 0), axis=1)

    any_ref = pl.BlockSpec(memory_space=pl.ANY)
    smem = pl.BlockSpec(memory_space=pltpu.SMEM)
    vmem = pl.BlockSpec(memory_space=pltpu.VMEM)
    spread = pl.pallas_call(
        ladder_kernel,
        out_shape=jax.ShapeDtypeStruct((CAP, n_cols * int_cols), jnp.bfloat16),
        in_specs=[smem, smem, vmem, vmem, any_ref, any_ref],
        out_specs=any_ref,
        scratch_shapes=[
            pltpu.VMEM((pair_rows, amp_cols), jnp.bfloat16),
            pltpu.VMEM((block_tiles, TILE, TILE), jnp.bfloat16),
            pltpu.VMEM((pair_rows, n_cols * amp_cols), jnp.bfloat16),
            [pltpu.VMEM((n_rows * count + 1, TILE, TILE), jnp.bfloat16) for count in GROUPS],
            pltpu.VMEM((n_rows * int_rows, CHUNK), jnp.bfloat16),
            pltpu.VMEM((n_cols * CAP, pair_rows), jnp.bfloat16),
            pltpu.VMEM((1, pair_rows), jnp.int32),
            pltpu.VMEM((pair_rows, CHUNK), jnp.float32),
            pltpu.VMEM((pair_rows, CHUNK), jnp.bfloat16),
            pltpu.VMEM((n_chunks, n_cols, CAP, CHUNK), jnp.bfloat16),
            pltpu.SemaphoreType.DMA((1 + n_tiles,)),
            pltpu.SemaphoreType.DMA((len(AMP_STEPS),)),
            pltpu.SemaphoreType.DMA((len(AMP_STEPS),)),
            pltpu.SemaphoreType.DMA((len(GROUPS), len(INT_STEPS))),
            pltpu.SemaphoreType.DMA((len(GROUPS), len(INT_STEPS))),
            pltpu.SemaphoreType.DMA((n_cols,)),
            pltpu.SemaphoreType.DMA((n_cols,)),
            pltpu.SemaphoreType.DMA((n_chunks,)),
        ],
        name="ladder",
        compiler_params=pltpu.CompilerParams(
            collective_id=0, has_side_effects=True, vmem_limit_bytes=56 * 1024 * 1024
        ),
    )(
        send_tiles, positions, amp_mask, pair_dest.reshape(1, pair_rows), amplitudes,
        integrals.reshape(k_tiles, TILE, int_cols),
    )
    parts_out = 8
    return pl.pallas_call(
        copy_kernel,
        out_shape=jax.ShapeDtypeStruct(spread.shape, spread.dtype),
        in_specs=[any_ref],
        out_specs=any_ref,
        scratch_shapes=[
            pltpu.VMEM((parts_out, CAP, n_cols * int_cols // parts_out), jnp.bfloat16),
            pltpu.SemaphoreType.DMA((parts_out,)),
            pltpu.SemaphoreType.DMA((parts_out,)),
        ],
        name="deliver",
    )(spread)


def solution(mesh):
    in_specs = (P("row", "col"), P("row", "col"), P("row", "col"), P(None, "col", None), P("row"))
    out_specs = P(("row", "col"), None)
    return jax.shard_map(
        on_device, mesh=mesh, in_specs=in_specs, out_specs=out_specs, check_vma=False
    )
```

```python
import functools

import jax
import jax.numpy as jnp
from jax import lax
from jax.experimental import pallas as pl
from jax.experimental.pallas import tpu as pltpu
from jax.sharding import PartitionSpec as P

TILE = 128
MESH = pl.DeviceIdType.MESH
CAP = 128
CHUNK_TILES = 2
CHUNK = CHUNK_TILES * TILE
GROUPS = (8, 8, 8, 8)
PART = 4

AMP_STEPS = {
    "x0": ((0, 0, 0), 0, (1, 0, 0)),
    "x1": ((0, 0, 0), 1, (1, 0, 0)),
    "p0": ((0, 0, 0), 0, (0, 1, 0)),
    "p1": ((0, 0, 0), 1, (0, 1, 0)),
    "m0": ((0, 0, 0), 0, (0, -1, 0)),
    "m1": ((0, 0, 0), 1, (0, -1, 0)),
    "pp": ((0, -1, 0), 0, (0, 1, 0)),
    "mm": ((0, 1, 0), 1, (0, -1, 0)),
    "xp0": ((1, 0, 0), 0, (0, 1, 0)),
    "xp1": ((1, 0, 0), 1, (0, 1, 0)),
    "xm0": ((1, 0, 0), 0, (0, -1, 0)),
    "xm1": ((1, 0, 0), 1, (0, -1, 0)),
    "xpp": ((1, -1, 0), 0, (0, 1, 0)),
    "xmm": ((1, 1, 0), 1, (0, -1, 0)),
    "c": ((0, 0, 0), None, (0, 0, 1)),
    "cp": ((0, -1, 0), None, (0, 0, 1)),
    "cm": ((0, 1, 0), None, (0, 0, 1)),
    "cq0": ((0, 2, 0), 0, (0, 0, 1)),
    "cq1": ((0, 2, 0), 1, (0, 0, 1)),
    "cx": ((1, 0, 0), None, (0, 0, 1)),
    "cxp": ((1, -1, 0), None, (0, 0, 1)),
    "cxm": ((1, 1, 0), None, (0, 0, 1)),
    "cxq0": ((1, 2, 0), 0, (0, 0, 1)),
    "cxq1": ((1, 2, 0), 1, (0, 0, 1)),
}
INT_STEPS = {
    "x": ((0, 0), None, (1, 0)),
    "p": ((0, 0), None, (0, 1)),
    "m": ((0, 0), None, (0, -1)),
    "pp": ((0, -1), 0, (0, 1)),
    "mm": ((0, 1), 1, (0, -1)),
    "xp": ((1, 0), None, (0, 1)),
    "xm": ((1, 0), None, (0, -1)),
    "xpp": ((1, -1), 0, (0, 1)),
    "xmm": ((1, 1), 1, (0, -1)),
}


def ladder_kernel(
    int_tiles, amp_mask, pair_dest, amp_hbm, int_hbm, out,
    amp_in, int_in, table_in, table, panel, comp, dense, select, key, acc, lad, stage,
    load_sem, table_sem, amp_send, amp_recv, int_send, int_recv, out_send, out_recv, own_sem,
):
    row, col = lax.axis_index("row"), lax.axis_index("col")
    n_cols = lax.axis_size("col")
    n_rows = lax.axis_size("row")
    pair_rows, amp_cols = amp_hbm.shape
    k_tiles, _, int_cols = int_hbm.shape
    n_tiles = int_cols // TILE
    n_chunks = n_tiles // CHUNK_TILES
    half_rows = pair_rows // 2

    core, y, x_hi = lax.rem(col, 2), lax.rem(lax.div(col, 2), 4), lax.div(col, 8)
    z, x_lo = lax.rem(row, 4), lax.div(row, 4)

    def col_at(dx, dy, dc):
        return lax.rem(x_hi + dx + 2, 2) * 8 + lax.rem(y + dy + 4, 4) * 2 + lax.rem(core + dc + 2, 2)

    def row_at(dx, dz):
        return lax.rem(x_lo + dx + 2, 2) * 4 + lax.rem(z + dz + 4, 4)

    load_amp = pltpu.make_async_copy(amp_hbm, amp_in, load_sem.at[0])
    load_amp.start()
    load_ints = [
        pltpu.make_async_copy(
            int_hbm.at[:, :, n * TILE:(n + 1) * TILE], int_in.at[n * k_tiles:(n + 1) * k_tiles], load_sem.at[1 + n]
        )
        for n in range(n_tiles)
    ]
    for load in load_ints:
        load.start()

    barrier = pltpu.get_barrier_semaphore()
    for step in range(1, n_cols):
        peer = lax.rem(col + step, n_cols)
        pl.semaphore_signal(barrier, inc=1, device_id=(row, peer), device_id_type=MESH)
    for dx, dz in ((1, 0), (0, 1), (0, -1)):
        pl.semaphore_signal(barrier, inc=1, device_id=(row_at(dx, dz), col), device_id_type=MESH)

    block_tiles = k_tiles * n_tiles
    slots = int_tiles.shape[1]
    lane = lax.broadcasted_iota(jnp.int32, (n_rows, TILE), 1)
    owner_row = lax.broadcasted_iota(jnp.int32, (n_rows, TILE), 0)
    tile_of = jnp.where(lane < block_tiles, lax.rem(lane, k_tiles) * n_tiles + lax.div(lane, k_tiles), -1)
    present = jnp.zeros((n_rows, TILE), jnp.int32)
    for r in range(n_rows):
        for s in range(slots):
            present = jnp.where((owner_row == r) & (tile_of == int_tiles[r, s]), 1, present)
    before_lane = lax.broadcasted_iota(jnp.int32, (TILE, TILE), 0) < lax.broadcasted_iota(jnp.int32, (TILE, TILE), 1)
    rank = jnp.dot(
        present.astype(jnp.float32).astype(jnp.bfloat16),
        jnp.where(before_lane, 1.0, 0.0).astype(jnp.bfloat16),
        preferred_element_type=jnp.float32,
    ).astype(jnp.int32)
    first = 0
    for g, count in enumerate(GROUPS):
        inside = (present == 1) & (rank >= first) & (rank < first + count)
        place = jnp.where(inside, owner_row * count + rank - first, n_rows * count)
        table_in[g * n_rows:(g + 1) * n_rows, :] = jnp.clip(place, 0, n_rows * count)
        first += count
    own_place = jnp.sum(
        jnp.where((owner_row == row) & (present == 1), rank + 1, 0).astype(jnp.float32), axis=0, keepdims=True
    )
    slot_at = lax.broadcasted_iota(jnp.int32, (slots, TILE), 0).astype(jnp.float32) + 1.0
    tile_at = lax.broadcasted_iota(jnp.int32, (slots, TILE), 1).astype(jnp.float32)
    own_tile = jnp.sum(jnp.where(own_place == slot_at, tile_at, 0.0), axis=1, keepdims=True)
    own_first = len(GROUPS) * n_rows
    table_in[own_first:own_first + slots, :] = jnp.clip(
        jnp.broadcast_to(own_tile, (slots, TILE)).astype(jnp.int32), 0, block_tiles - 1
    )
    load_table = pltpu.make_async_copy(table_in, table, table_sem)
    load_table.start()

    def amp_copy(name, seen_by_receiver):
        what, half, to = AMP_STEPS[name]
        sem = list(AMP_STEPS).index(name)
        owner = col_at(*(w - t for w, t in zip(what, to))) if seen_by_receiver else col_at(*what)
        at = pl.ds(pl.multiple_of(owner * amp_cols, amp_cols), amp_cols)
        piece = panel.at[:, at] if half is None else panel.at[half * half_rows:(half + 1) * half_rows, at]
        return pltpu.make_async_remote_copy(
            piece, piece, amp_send.at[sem], amp_recv.at[sem], device_id=(row, col_at(*to)), device_id_type=MESH
        )

    def int_copy(g, name, seen_by_receiver):
        what, half, to = INT_STEPS[name]
        sem = list(INT_STEPS).index(name)
        owner = row_at(*(w - t for w, t in zip(what, to))) if seen_by_receiver else row_at(*what)
        count = GROUPS[g]
        if half is None:
            piece = comp[g].at[pl.ds(owner * count, count)]
        else:
            piece = comp[g].at[pl.ds(owner * count + half * (count // 2), count // 2)]
        return pltpu.make_async_remote_copy(
            piece, piece, int_send.at[g, sem], int_recv.at[g, sem], device_id=(row_at(*to), col), device_id_type=MESH
        )

    def amp_start(*names):
        for name in names:
            amp_copy(name, False).start()

    def amp_arrived(*names):
        for name in names:
            amp_copy(name, True).wait_recv()

    def int_start(g, *names):
        for name in names:
            int_copy(g, name, False).start()

    def int_arrived(g, *names):
        for name in names:
            int_copy(g, name, True).wait_recv()

    load_amp.wait()
    own_cols = pl.multiple_of(col * amp_cols, amp_cols)
    kept = amp_mask[...].astype(jnp.float32).astype(jnp.bfloat16)
    for a in range(pair_rows // TILE):
        for k in range(amp_cols // TILE):
            tile = amp_in[a * TILE:(a + 1) * TILE, k * TILE:(k + 1) * TILE]
            panel[a * TILE:(a + 1) * TILE, pl.ds(own_cols + k * TILE, TILE)] = tile * kept[k:k + 1, a:a + 1]
    pl.semaphore_wait(barrier, n_cols - 1 + 3)
    amp_start("x0", "p0", "m1", "x1", "p1", "m0", "c")

    load_table.wait()
    for load in load_ints:
        load.wait()
    first = 0
    for g, count in enumerate(GROUPS):
        for slot in range(count):
            comp[g][row * count + slot] = int_in[table[own_first + first + slot, 0]]
        comp[g][n_rows * count] = jnp.zeros((TILE, TILE), jnp.bfloat16)
        first += count
    int_start(0, "x", "p", "m")
    int_start(1, "p", "m")

    dest_all = lax.broadcasted_iota(jnp.int32, (n_cols, pair_rows), 0)
    onehot = jnp.where(dest_all == pair_dest[...], 1.0, 0.0)
    for block in range(pair_rows // TILE):
        cols = slice(block * TILE, (block + 1) * TILE)
        q = lax.broadcasted_iota(jnp.int32, (pair_rows, TILE), 0)
        p = lax.broadcasted_iota(jnp.int32, (pair_rows, TILE), 1) + block * TILE
        earlier = jnp.where(q < p, 1.0, 0.0).astype(jnp.bfloat16)
        before = jnp.dot(onehot.astype(jnp.bfloat16), earlier, preferred_element_type=jnp.float32)
        slot = jnp.sum(before * onehot[:, cols], axis=0, keepdims=True)
        ahead = pair_dest[:, cols] - col
        key[:, cols] = jnp.where(ahead < 0, ahead + n_cols, ahead) * CAP + slot.astype(jnp.int32)

    def fill_select(d, carry):
        places = lax.broadcasted_iota(jnp.int32, (CAP, pair_rows), 0) + d * CAP
        at = pl.ds(pl.multiple_of(d * CAP, CAP), CAP)
        select[at, :] = jnp.where(places == key[...], 1.0, 0.0).astype(jnp.bfloat16)
        return carry

    lax.fori_loop(0, n_cols, fill_select, 0)

    def unpack(q, groups):
        def one_row(r, carry):
            for n in range(CHUNK_TILES):
                for k in range(k_tiles):
                    tile = None
                    for g in range(groups):
                        at = table[g * n_rows + r, (q * CHUNK_TILES + n) * k_tiles + k]
                        part = comp[g][at]
                        tile = part if tile is None else tile + part
                    down = pl.ds(pl.multiple_of((r * k_tiles + k) * TILE, TILE), TILE)
                    dense[down, n * TILE:(n + 1) * TILE] = tile
            return carry

        lax.fori_loop(0, n_rows, one_row, 0)

    def multiply(start, depth, first, last):
        m_rows = pair_rows // 2

        def one_half(m, carry):
            at = pl.ds(pl.multiple_of(m * m_rows, m_rows), m_rows)
            deep = pl.ds(pl.multiple_of(start, 512), depth)
            total = jnp.dot(panel[at, deep], dense[deep, :], preferred_element_type=jnp.float32)
            if not first:
                total = total + acc[at, :]
            if last:
                lad[at, :] = total.astype(jnp.bfloat16)
            else:
                acc[at, :] = total
            return carry

        lax.fori_loop(0, 2, one_half, 0)

    def out_piece(owner, q):
        return out.at[:, pl.ds(pl.multiple_of(owner * int_cols + q * CHUNK, CHUNK), CHUNK)]

    def send_part(q, j):
        for i in range(PART):
            step = j * PART + i
            peer = lax.rem(col + step, n_cols)

            def to_peer():
                pltpu.make_async_remote_copy(
                    stage.at[q, step], out_piece(col, q), out_send.at[step], out_recv.at[step],
                    device_id=(row, peer), device_id_type=MESH,
                ).start()

            if step == 0:
                pltpu.make_async_copy(stage.at[q, 0], out_piece(col, q), own_sem.at[q]).start()
            else:
                to_peer()

    n_parts = n_cols // PART

    def spread(q):
        for j in range(n_parts):
            at = slice(j * PART * CAP, (j + 1) * PART * CAP)
            rows = jnp.dot(select[at, :], lad[...], preferred_element_type=jnp.float32).astype(jnp.bfloat16)
            stage[q, j * PART:(j + 1) * PART] = rows.reshape(PART, CAP, CHUNK)
            if j > 0:
                send_part(q, j - 1)

    def chunks(lo, hi, groups):
        def one_chunk(q, carry):
            unpack(q, groups)
            send_part(q - 1, n_parts - 1)
            multiply(0, n_cols * amp_cols, True, True)
            spread(q)
            return carry

        lax.fori_loop(lo, hi, one_chunk, 0)

    amp_arrived("p0", "m1")
    amp_start("pp", "mm")
    int_arrived(0, "p", "m")
    int_start(0, "pp", "mm")
    amp_arrived("x0", "x1")
    amp_start("xp0", "xm1", "xp1", "xm0", "cx")
    int_start(1, "x")
    amp_arrived("p1", "m0")
    amp_start("cp", "cm")
    int_arrived(1, "p", "m")
    int_start(1, "pp", "mm")
    amp_arrived("pp", "mm")
    amp_start("cq0", "cq1")
    int_arrived(0, "x")
    int_start(0, "xp", "xm")
    int_start(2, "x")
    amp_arrived("xp0", "xm1")
    amp_start("xpp", "xmm")
    int_arrived(0, "xp", "xm")
    int_start(0, "xpp", "xmm")
    int_start(3, "x")
    int_arrived(1, "x")
    int_start(1, "xp", "xm")
    int_start(2, "p", "m")
    amp_arrived("c", "cp", "cm", "cq0", "cq1")
    amp_arrived("xp1", "xm0")
    amp_start("cxp", "cxm")
    int_arrived(0, "pp", "mm", "xpp", "xmm")

    y_cols = 2 * amp_cols
    x_cols = 4 * y_cols
    far = lax.rem(x_hi + 1, 2) * x_cols
    unpack(0, 1)
    multiply(x_hi * x_cols, x_cols, True, False)
    amp_arrived("cx")
    multiply(far + y * y_cols, y_cols, False, False)
    amp_arrived("xpp")
    amp_start("cxq0")
    amp_arrived("xmm")
    amp_start("cxq1")
    int_arrived(1, "xp", "xm")
    int_start(1, "xpp", "xmm")
    amp_arrived("cxp")
    multiply(far + lax.rem(y + 3, 4) * y_cols, y_cols, False, False)
    amp_arrived("cxm")
    multiply(far + lax.rem(y + 1, 4) * y_cols, y_cols, False, False)
    amp_arrived("cxq0", "cxq1")
    multiply(far + lax.rem(y + 2, 4) * y_cols, y_cols, False, True)
    spread(0)

    int_arrived(2, "x")
    int_start(2, "xp", "xm")
    int_arrived(2, "p", "m")
    int_start(2, "pp", "mm")
    int_start(3, "p", "m")
    int_arrived(1, "pp", "mm", "xpp", "xmm")
    chunks(1, 2, 2)
    int_arrived(2, "xp", "xm")
    int_start(2, "xpp", "xmm")
    int_arrived(3, "x")
    int_start(3, "xp", "xm")
    int_arrived(3, "p", "m")
    int_start(3, "pp", "mm")
    int_arrived(2, "pp", "mm", "xpp", "xmm")
    chunks(2, 3, 3)
    int_arrived(3, "xp", "xm")
    int_start(3, "xpp", "xmm")
    int_arrived(3, "pp", "mm", "xpp", "xmm")
    chunks(3, n_chunks, 4)

    for name in AMP_STEPS:
        amp_copy(name, False).wait_send()
    send_part(n_chunks - 1, n_parts - 1)
    for g in range(len(GROUPS)):
        for name in INT_STEPS:
            int_copy(g, name, False).wait_send()

    def own_done(q, carry):
        pltpu.make_async_copy(stage.at[q, 0], out_piece(col, q), own_sem.at[q]).wait()
        return carry

    lax.fori_loop(0, n_chunks, own_done, 0)

    def peer_done(step, carry):
        source = lax.rem(col - step + n_cols, n_cols)
        block = out.at[:, pl.ds(pl.multiple_of(source * int_cols, int_cols), int_cols)]
        whole = pltpu.make_async_remote_copy(
            block, block, out_send.at[step], out_recv.at[step], device_id=(row, source), device_id_type=MESH
        )
        whole.wait()
        return carry

    lax.fori_loop(1, n_cols, peer_done, 0)


def copy_kernel(src, dst, sem):
    rows = TILE // sem.shape[0]
    writes = [
        pltpu.make_async_copy(src.at[i * rows:(i + 1) * rows], dst.at[i * rows:(i + 1) * rows], sem.at[i])
        for i in range(sem.shape[0])
    ]
    for write in writes:
        write.start()
    for write in writes:
        write.wait()


def on_device(amplitudes, amp_mask, integrals, int_tiles, pair_dest):
    pair_rows, amp_cols = amplitudes.shape
    int_rows, int_cols = integrals.shape
    n_rows, n_cols = lax.axis_size("row"), lax.axis_size("col")
    k_tiles, n_tiles = int_rows // TILE, int_cols // TILE
    block_tiles = k_tiles * n_tiles
    slots = int_tiles.shape[2]
    n_chunks = n_tiles // CHUNK_TILES

    any_ref = pl.BlockSpec(memory_space=pl.ANY)
    hbm = pl.BlockSpec(memory_space=pltpu.HBM)
    smem = pl.BlockSpec(memory_space=pltpu.SMEM)
    vmem = pl.BlockSpec(memory_space=pltpu.VMEM)
    spread = pl.pallas_call(
        ladder_kernel,
        out_shape=pltpu.VMEM((CAP, n_cols * int_cols), jnp.bfloat16),
        in_specs=[smem, vmem, vmem, hbm, hbm],
        out_specs=vmem,
        scratch_shapes=[
            pltpu.VMEM((pair_rows, amp_cols), jnp.bfloat16),
            pltpu.VMEM((block_tiles, TILE, TILE), jnp.bfloat16),
            pltpu.VMEM((len(GROUPS) * n_rows + slots, TILE), jnp.int32),
            pltpu.SMEM((len(GROUPS) * n_rows + slots, TILE), jnp.int32),
            pltpu.VMEM((pair_rows, n_cols * amp_cols), jnp.bfloat16),
            [pltpu.VMEM((n_rows * count + 1, TILE, TILE), jnp.bfloat16) for count in GROUPS],
            pltpu.VMEM((n_rows * int_rows, CHUNK), jnp.bfloat16),
            pltpu.VMEM((n_cols * CAP, pair_rows), jnp.bfloat16),
            pltpu.VMEM((1, pair_rows), jnp.int32),
            pltpu.VMEM((pair_rows, CHUNK), jnp.float32),
            pltpu.VMEM((pair_rows, CHUNK), jnp.bfloat16),
            pltpu.VMEM((n_chunks, n_cols, CAP, CHUNK), jnp.bfloat16),
            pltpu.SemaphoreType.DMA((1 + n_tiles,)),
            pltpu.SemaphoreType.DMA,
            pltpu.SemaphoreType.DMA((len(AMP_STEPS),)),
            pltpu.SemaphoreType.DMA((len(AMP_STEPS),)),
            pltpu.SemaphoreType.DMA((len(GROUPS), len(INT_STEPS))),
            pltpu.SemaphoreType.DMA((len(GROUPS), len(INT_STEPS))),
            pltpu.SemaphoreType.DMA((n_cols,)),
            pltpu.SemaphoreType.DMA((n_cols,)),
            pltpu.SemaphoreType.DMA((n_chunks,)),
        ],
        name="ladder",
        compiler_params=pltpu.CompilerParams(
            collective_id=0, has_side_effects=True, vmem_limit_bytes=111 * 512 * 1024
        ),
    )(
        int_tiles.reshape(n_rows, slots), amp_mask.T, pair_dest.reshape(1, pair_rows), amplitudes,
        integrals.reshape(k_tiles, TILE, int_cols),
    )
    return pl.pallas_call(
        copy_kernel,
        out_shape=jax.ShapeDtypeStruct(spread.shape, spread.dtype),
        in_specs=[vmem],
        out_specs=any_ref,
        scratch_shapes=[pltpu.SemaphoreType.DMA((8,))],
        name="deliver",
        compiler_params=pltpu.CompilerParams(vmem_limit_bytes=4 * 1024 * 1024),
    )(spread)


def solution(mesh):
    in_specs = (P("row", "col"), P("row", "col"), P("row", "col"), P(None, "col", None), P("row"))
    out_specs = P(("row", "col"), None)
    return jax.shard_map(
        on_device, mesh=mesh, in_specs=in_specs, out_specs=out_specs, check_vma=False
    )
```

```python
import functools

import jax
import jax.numpy as jnp
from jax import lax
from jax.experimental import pallas as pl
from jax.experimental.pallas import tpu as pltpu
from jax.sharding import PartitionSpec as P

TILE = 128
MESH = pl.DeviceIdType.MESH
CAP = 128
CHUNK_TILES = 2
CHUNK = CHUNK_TILES * TILE
GROUPS = (8, 8, 8, 8)
PART = 2
FIRST_STEP = 10

AMP_STEPS = {
    "x0": ((0, 0, 0), 0, (1, 0, 0)),
    "x1": ((0, 0, 0), 1, (1, 0, 0)),
    "p0": ((0, 0, 0), 0, (0, 1, 0)),
    "p1": ((0, 0, 0), 1, (0, 1, 0)),
    "m0": ((0, 0, 0), 0, (0, -1, 0)),
    "m1": ((0, 0, 0), 1, (0, -1, 0)),
    "pp": ((0, -1, 0), 0, (0, 1, 0)),
    "mm": ((0, 1, 0), 1, (0, -1, 0)),
    "xp0": ((1, 0, 0), 0, (0, 1, 0)),
    "xp1": ((1, 0, 0), 1, (0, 1, 0)),
    "xm0": ((1, 0, 0), 0, (0, -1, 0)),
    "xm1": ((1, 0, 0), 1, (0, -1, 0)),
    "xpp": ((1, -1, 0), 0, (0, 1, 0)),
    "xmm": ((1, 1, 0), 1, (0, -1, 0)),
    "c": ((0, 0, 0), None, (0, 0, 1)),
    "cp": ((0, -1, 0), None, (0, 0, 1)),
    "cm": ((0, 1, 0), None, (0, 0, 1)),
    "cq0": ((0, 2, 0), 0, (0, 0, 1)),
    "cq1": ((0, 2, 0), 1, (0, 0, 1)),
    "cx": ((1, 0, 0), None, (0, 0, 1)),
    "cxp": ((1, -1, 0), None, (0, 0, 1)),
    "cxm": ((1, 1, 0), None, (0, 0, 1)),
    "cxq0": ((1, 2, 0), 0, (0, 0, 1)),
    "cxq1": ((1, 2, 0), 1, (0, 0, 1)),
}
INT_STEPS = {
    "x": ((0, 0), None, (1, 0)),
    "p": ((0, 0), None, (0, 1)),
    "m": ((0, 0), None, (0, -1)),
    "pp": ((0, -1), 0, (0, 1)),
    "mm": ((0, 1), 1, (0, -1)),
    "xp": ((1, 0), None, (0, 1)),
    "xm": ((1, 0), None, (0, -1)),
    "xpp": ((1, -1), 0, (0, 1)),
    "xmm": ((1, 1), 1, (0, -1)),
}


def ladder_kernel(
    int_tiles, amp_mask, pair_dest, amp_hbm, int_hbm, out,
    amp_in, int_in, table_in, table, panel, comp, dense, select, key, acc, lad, stage,
    load_sem, table_sem, amp_send, amp_recv, int_send, int_recv, out_send, out_recv, own_sem,
):
    row, col = lax.axis_index("row"), lax.axis_index("col")
    n_cols = lax.axis_size("col")
    n_rows = lax.axis_size("row")
    pair_rows, amp_cols = amp_hbm.shape
    k_tiles, _, int_cols = int_hbm.shape
    n_tiles = int_cols // TILE
    n_chunks = n_tiles // CHUNK_TILES
    half_rows = pair_rows // 2

    core, y, x_hi = lax.rem(col, 2), lax.rem(lax.div(col, 2), 4), lax.div(col, 8)
    z, x_lo = lax.rem(row, 4), lax.div(row, 4)

    def col_at(dx, dy, dc):
        return lax.rem(x_hi + dx + 2, 2) * 8 + lax.rem(y + dy + 4, 4) * 2 + lax.rem(core + dc + 2, 2)

    def row_at(dx, dz):
        return lax.rem(x_lo + dx + 2, 2) * 4 + lax.rem(z + dz + 4, 4)

    load_amp = pltpu.make_async_copy(amp_hbm, amp_in, load_sem.at[0])
    load_amp.start()
    load_ints = [
        pltpu.make_async_copy(
            int_hbm.at[:, :, n * TILE:(n + 1) * TILE], int_in.at[n * k_tiles:(n + 1) * k_tiles], load_sem.at[1 + n]
        )
        for n in range(n_tiles)
    ]
    for load in load_ints:
        load.start()

    barrier = pltpu.get_barrier_semaphore()
    for step in range(1, n_cols):
        peer = lax.rem(col + step, n_cols)
        pl.semaphore_signal(barrier, inc=1, device_id=(row, peer), device_id_type=MESH)
    for dx, dz in ((1, 0), (0, 1), (0, -1)):
        pl.semaphore_signal(barrier, inc=1, device_id=(row_at(dx, dz), col), device_id_type=MESH)

    block_tiles = k_tiles * n_tiles
    slots = int_tiles.shape[1]
    lane = lax.broadcasted_iota(jnp.int32, (n_rows, TILE), 1)
    owner_row = lax.broadcasted_iota(jnp.int32, (n_rows, TILE), 0)
    tile_of = jnp.where(lane < block_tiles, lax.rem(lane, k_tiles) * n_tiles + lax.div(lane, k_tiles), -1)
    present = jnp.zeros((n_rows, TILE), jnp.int32)
    for r in range(n_rows):
        for s in range(slots):
            present = jnp.where((owner_row == r) & (tile_of == int_tiles[r, s]), 1, present)
    before_lane = lax.broadcasted_iota(jnp.int32, (TILE, TILE), 0) < lax.broadcasted_iota(jnp.int32, (TILE, TILE), 1)
    rank = jnp.dot(
        present.astype(jnp.float32).astype(jnp.bfloat16),
        jnp.where(before_lane, 1.0, 0.0).astype(jnp.bfloat16),
        preferred_element_type=jnp.float32,
    ).astype(jnp.int32)
    first = 0
    for g, count in enumerate(GROUPS):
        inside = (present == 1) & (rank >= first) & (rank < first + count)
        place = jnp.where(inside, owner_row * count + rank - first, n_rows * count)
        table_in[g * n_rows:(g + 1) * n_rows, :] = jnp.clip(place, 0, n_rows * count)
        first += count
    own_place = jnp.sum(
        jnp.where((owner_row == row) & (present == 1), rank + 1, 0).astype(jnp.float32), axis=0, keepdims=True
    )
    slot_at = lax.broadcasted_iota(jnp.int32, (slots, TILE), 0).astype(jnp.float32) + 1.0
    tile_at = lax.broadcasted_iota(jnp.int32, (slots, TILE), 1).astype(jnp.float32)
    own_tile = jnp.sum(jnp.where(own_place == slot_at, tile_at, 0.0), axis=1, keepdims=True)
    own_first = len(GROUPS) * n_rows
    table_in[own_first:own_first + slots, :] = jnp.clip(
        jnp.broadcast_to(own_tile, (slots, TILE)).astype(jnp.int32), 0, block_tiles - 1
    )
    load_table = pltpu.make_async_copy(table_in, table, table_sem)
    load_table.start()

    def amp_copy(name, seen_by_receiver):
        what, half, to = AMP_STEPS[name]
        sem = list(AMP_STEPS).index(name)
        owner = col_at(*(w - t for w, t in zip(what, to))) if seen_by_receiver else col_at(*what)
        at = pl.ds(pl.multiple_of(owner * amp_cols, amp_cols), amp_cols)
        piece = panel.at[:, at] if half is None else panel.at[half * half_rows:(half + 1) * half_rows, at]
        return pltpu.make_async_remote_copy(
            piece, piece, amp_send.at[sem], amp_recv.at[sem], device_id=(row, col_at(*to)), device_id_type=MESH
        )

    def int_copy(g, name, seen_by_receiver):
        what, half, to = INT_STEPS[name]
        sem = list(INT_STEPS).index(name)
        owner = row_at(*(w - t for w, t in zip(what, to))) if seen_by_receiver else row_at(*what)
        count = GROUPS[g]
        if half is None:
            piece = comp[g].at[pl.ds(owner * count, count)]
        else:
            piece = comp[g].at[pl.ds(owner * count + half * (count // 2), count // 2)]
        return pltpu.make_async_remote_copy(
            piece, piece, int_send.at[g, sem], int_recv.at[g, sem], device_id=(row_at(*to), col), device_id_type=MESH
        )

    def amp_start(*names):
        for name in names:
            amp_copy(name, False).start()

    def amp_arrived(*names):
        for name in names:
            amp_copy(name, True).wait_recv()

    def int_start(g, *names):
        for name in names:
            int_copy(g, name, False).start()

    def int_arrived(g, *names):
        for name in names:
            int_copy(g, name, True).wait_recv()

    load_amp.wait()
    own_cols = pl.multiple_of(col * amp_cols, amp_cols)
    kept = amp_mask[...].astype(jnp.float32).astype(jnp.bfloat16)
    for a in range(pair_rows // TILE):
        for k in range(amp_cols // TILE):
            tile = amp_in[a * TILE:(a + 1) * TILE, k * TILE:(k + 1) * TILE]
            panel[a * TILE:(a + 1) * TILE, pl.ds(own_cols + k * TILE, TILE)] = tile * kept[k:k + 1, a:a + 1]
    pl.semaphore_wait(barrier, n_cols - 1 + 3)
    amp_start("x0", "p0", "m1", "x1", "p1", "m0", "c")

    load_table.wait()
    for load in load_ints:
        load.wait()
    first = 0
    for g, count in enumerate(GROUPS):
        for slot in range(count):
            comp[g][row * count + slot] = int_in[table[own_first + first + slot, 0]]
        comp[g][n_rows * count] = jnp.zeros((TILE, TILE), jnp.bfloat16)
        first += count
    int_start(0, "x", "p", "m")
    int_start(1, "p", "m")

    dest_all = lax.broadcasted_iota(jnp.int32, (n_cols, pair_rows), 0)
    onehot = jnp.where(dest_all == pair_dest[...], 1.0, 0.0)
    for block in range(pair_rows // TILE):
        cols = slice(block * TILE, (block + 1) * TILE)
        q = lax.broadcasted_iota(jnp.int32, (pair_rows, TILE), 0)
        p = lax.broadcasted_iota(jnp.int32, (pair_rows, TILE), 1) + block * TILE
        earlier = jnp.where(q < p, 1.0, 0.0).astype(jnp.bfloat16)
        before = jnp.dot(onehot.astype(jnp.bfloat16), earlier, preferred_element_type=jnp.float32)
        slot = jnp.sum(before * onehot[:, cols], axis=0, keepdims=True)
        ahead = pair_dest[:, cols] - col - FIRST_STEP + n_cols
        ahead = jnp.where(ahead < 0, ahead + n_cols, ahead)
        key[:, cols] = jnp.where(ahead >= n_cols, ahead - n_cols, ahead) * CAP + slot.astype(jnp.int32)

    def fill_select(d, carry):
        places = lax.broadcasted_iota(jnp.int32, (CAP, pair_rows), 0) + d * CAP
        at = pl.ds(pl.multiple_of(d * CAP, CAP), CAP)
        select[at, :] = jnp.where(places == key[...], 1.0, 0.0).astype(jnp.bfloat16)
        return carry

    lax.fori_loop(0, n_cols, fill_select, 0)

    def unpack(q, groups):
        def one_row(r, carry):
            for n in range(CHUNK_TILES):
                for k in range(k_tiles):
                    tile = None
                    for g in range(groups):
                        at = table[g * n_rows + r, (q * CHUNK_TILES + n) * k_tiles + k]
                        part = comp[g][at]
                        tile = part if tile is None else tile + part
                    down = pl.ds(pl.multiple_of((r * k_tiles + k) * TILE, TILE), TILE)
                    dense[down, n * TILE:(n + 1) * TILE] = tile
            return carry

        lax.fori_loop(0, n_rows, one_row, 0)

    def multiply(start, depth, first, last):
        m_rows = pair_rows // 2

        def one_half(m, carry):
            at = pl.ds(pl.multiple_of(m * m_rows, m_rows), m_rows)
            deep = pl.ds(pl.multiple_of(start, 512), depth)
            total = jnp.dot(panel[at, deep], dense[deep, :], preferred_element_type=jnp.float32)
            if not first:
                total = total + acc[at, :]
            if last:
                lad[at, :] = total.astype(jnp.bfloat16)
            else:
                acc[at, :] = total
            return carry

        lax.fori_loop(0, 2, one_half, 0)

    def out_piece(owner, q):
        return out.at[:, pl.ds(pl.multiple_of(owner * int_cols + q * CHUNK, CHUNK), CHUNK)]

    n_parts = n_cols // PART
    own_place_at = n_cols - FIRST_STEP

    def send_part(q, j):
        for place in range(j * PART, (j + 1) * PART):
            step = (place + FIRST_STEP) % n_cols
            peer = lax.rem(col + step, n_cols)

            def to_peer():
                pltpu.make_async_remote_copy(
                    stage.at[q, place], out_piece(col, q), out_send.at[step], out_recv.at[step],
                    device_id=(row, peer), device_id_type=MESH,
                ).start()

            if step == 0:
                pltpu.make_async_copy(stage.at[q, own_place_at], out_piece(col, q), own_sem.at[q]).start()
            else:
                to_peer()


    def spread(q):
        for j in range(n_parts):
            at = slice(j * PART * CAP, (j + 1) * PART * CAP)
            rows = jnp.dot(select[at, :], lad[...], preferred_element_type=jnp.float32).astype(jnp.bfloat16)
            stage[q, j * PART:(j + 1) * PART] = rows.reshape(PART, CAP, CHUNK)
            if j > 0:
                send_part(q, j - 1)

    def chunks(lo, hi, groups):
        def one_chunk(q, carry):
            unpack(q, groups)
            send_part(q - 1, n_parts - 1)
            multiply(0, n_cols * amp_cols, True, True)
            spread(q)
            return carry

        lax.fori_loop(lo, hi, one_chunk, 0)

    amp_arrived("p0", "m1")
    amp_start("pp", "mm")
    int_arrived(0, "p", "m")
    int_start(0, "pp", "mm")
    amp_arrived("x0", "x1")
    amp_start("xp0", "xm1", "xp1", "xm0", "cx")
    int_start(1, "x")
    amp_arrived("p1", "m0")
    amp_start("cp", "cm")
    int_arrived(1, "p", "m")
    int_start(1, "pp", "mm")
    amp_arrived("pp", "mm")
    amp_start("cq0", "cq1")
    int_arrived(0, "x")
    int_start(0, "xp", "xm")
    int_start(2, "x")
    amp_arrived("xp0", "xm1")
    amp_start("xpp", "xmm")
    int_arrived(0, "xp", "xm")
    int_start(0, "xpp", "xmm")
    int_start(3, "x")
    int_arrived(1, "x")
    int_start(1, "xp", "xm")
    int_start(2, "p", "m")
    amp_arrived("c", "cp", "cm", "cq0", "cq1")
    amp_arrived("xp1", "xm0")
    amp_start("cxp", "cxm")
    int_arrived(0, "pp", "mm", "xpp", "xmm")

    y_cols = 2 * amp_cols
    x_cols = 4 * y_cols
    far = lax.rem(x_hi + 1, 2) * x_cols
    unpack(0, 1)
    multiply(x_hi * x_cols, x_cols, True, False)
    amp_arrived("cx")
    multiply(far + y * y_cols, y_cols, False, False)
    amp_arrived("xpp")
    amp_start("cxq0")
    amp_arrived("xmm")
    amp_start("cxq1")
    int_arrived(1, "xp", "xm")
    int_start(1, "xpp", "xmm")
    int_arrived(2, "x")
    int_start(2, "xp", "xm")
    amp_arrived("cxp")
    multiply(far + lax.rem(y + 3, 4) * y_cols, y_cols, False, False)
    amp_arrived("cxm")
    multiply(far + lax.rem(y + 1, 4) * y_cols, y_cols, False, False)
    amp_arrived("cxq0", "cxq1")
    multiply(far + lax.rem(y + 2, 4) * y_cols, y_cols, False, True)
    spread(0)

    int_arrived(2, "p", "m")
    int_start(2, "pp", "mm")
    int_start(3, "p", "m")
    int_arrived(1, "pp", "mm", "xpp", "xmm")
    chunks(1, 2, 2)
    int_arrived(2, "xp", "xm")
    int_start(2, "xpp", "xmm")
    int_arrived(3, "x")
    int_start(3, "xp", "xm")
    int_arrived(3, "p", "m")
    int_start(3, "pp", "mm")
    int_arrived(2, "pp", "mm", "xpp", "xmm")
    chunks(2, 3, 3)
    int_arrived(3, "xp", "xm")
    int_start(3, "xpp", "xmm")
    int_arrived(3, "pp", "mm", "xpp", "xmm")
    chunks(3, n_chunks, 4)

    for name in AMP_STEPS:
        amp_copy(name, False).wait_send()
    send_part(n_chunks - 1, n_parts - 1)
    for g in range(len(GROUPS)):
        for name in INT_STEPS:
            int_copy(g, name, False).wait_send()

    def own_done(q, carry):
        pltpu.make_async_copy(stage.at[q, own_place_at], out_piece(col, q), own_sem.at[q]).wait()
        return carry

    lax.fori_loop(0, n_chunks, own_done, 0)

    def peer_done(step, carry):
        source = lax.rem(col - step + n_cols, n_cols)
        block = out.at[:, pl.ds(pl.multiple_of(source * int_cols, int_cols), int_cols)]
        whole = pltpu.make_async_remote_copy(
            block, block, out_send.at[step], out_recv.at[step], device_id=(row, source), device_id_type=MESH
        )
        whole.wait()
        return carry

    lax.fori_loop(1, n_cols, peer_done, 0)


def copy_kernel(src, dst, sem):
    rows = TILE // sem.shape[0]
    writes = [
        pltpu.make_async_copy(src.at[i * rows:(i + 1) * rows], dst.at[i * rows:(i + 1) * rows], sem.at[i])
        for i in range(sem.shape[0])
    ]
    for write in writes:
        write.start()
    for write in writes:
        write.wait()


def on_device(amplitudes, amp_mask, integrals, int_tiles, pair_dest):
    pair_rows, amp_cols = amplitudes.shape
    int_rows, int_cols = integrals.shape
    n_rows, n_cols = lax.axis_size("row"), lax.axis_size("col")
    k_tiles, n_tiles = int_rows // TILE, int_cols // TILE
    block_tiles = k_tiles * n_tiles
    slots = int_tiles.shape[2]
    n_chunks = n_tiles // CHUNK_TILES

    any_ref = pl.BlockSpec(memory_space=pl.ANY)
    hbm = pl.BlockSpec(memory_space=pltpu.HBM)
    smem = pl.BlockSpec(memory_space=pltpu.SMEM)
    vmem = pl.BlockSpec(memory_space=pltpu.VMEM)
    spread = pl.pallas_call(
        ladder_kernel,
        out_shape=pltpu.VMEM((CAP, n_cols * int_cols), jnp.bfloat16),
        in_specs=[smem, vmem, vmem, hbm, hbm],
        out_specs=vmem,
        scratch_shapes=[
            pltpu.VMEM((pair_rows, amp_cols), jnp.bfloat16),
            pltpu.VMEM((block_tiles, TILE, TILE), jnp.bfloat16),
            pltpu.VMEM((len(GROUPS) * n_rows + slots, TILE), jnp.int32),
            pltpu.SMEM((len(GROUPS) * n_rows + slots, TILE), jnp.int32),
            pltpu.VMEM((pair_rows, n_cols * amp_cols), jnp.bfloat16),
            [pltpu.VMEM((n_rows * count + 1, TILE, TILE), jnp.bfloat16) for count in GROUPS],
            pltpu.VMEM((n_rows * int_rows, CHUNK), jnp.bfloat16),
            pltpu.VMEM((n_cols * CAP, pair_rows), jnp.bfloat16),
            pltpu.VMEM((1, pair_rows), jnp.int32),
            pltpu.VMEM((pair_rows, CHUNK), jnp.float32),
            pltpu.VMEM((pair_rows, CHUNK), jnp.bfloat16),
            pltpu.VMEM((n_chunks, n_cols, CAP, CHUNK), jnp.bfloat16),
            pltpu.SemaphoreType.DMA((1 + n_tiles,)),
            pltpu.SemaphoreType.DMA,
            pltpu.SemaphoreType.DMA((len(AMP_STEPS),)),
            pltpu.SemaphoreType.DMA((len(AMP_STEPS),)),
            pltpu.SemaphoreType.DMA((len(GROUPS), len(INT_STEPS))),
            pltpu.SemaphoreType.DMA((len(GROUPS), len(INT_STEPS))),
            pltpu.SemaphoreType.DMA((n_cols,)),
            pltpu.SemaphoreType.DMA((n_cols,)),
            pltpu.SemaphoreType.DMA((n_chunks,)),
        ],
        name="ladder",
        compiler_params=pltpu.CompilerParams(
            collective_id=0, has_side_effects=True, vmem_limit_bytes=111 * 512 * 1024
        ),
    )(
        int_tiles.reshape(n_rows, slots), amp_mask.T, pair_dest.reshape(1, pair_rows), amplitudes,
        integrals.reshape(k_tiles, TILE, int_cols),
    )
    return pl.pallas_call(
        copy_kernel,
        out_shape=jax.ShapeDtypeStruct(spread.shape, spread.dtype),
        in_specs=[vmem],
        out_specs=any_ref,
        scratch_shapes=[pltpu.SemaphoreType.DMA((8,))],
        name="deliver",
        compiler_params=pltpu.CompilerParams(vmem_limit_bytes=4 * 1024 * 1024),
    )(spread)


def solution(mesh):
    in_specs = (P("row", "col"), P("row", "col"), P("row", "col"), P(None, "col", None), P("row"))
    out_specs = P(("row", "col"), None)
    return jax.shard_map(
        on_device, mesh=mesh, in_specs=in_specs, out_specs=out_specs, check_vma=False
    )
```

```python
import functools

import jax
import jax.numpy as jnp
from jax import lax
from jax.experimental import pallas as pl
from jax.experimental.pallas import tpu as pltpu
from jax.sharding import PartitionSpec as P

TILE = 128
MESH = pl.DeviceIdType.MESH
CAP = 128
CHUNK_TILES = 2
CHUNK = CHUNK_TILES * TILE
GROUPS = (8, 8, 8, 8)
PART = 2
FIRST_STEP = 9

AMP_STEPS = {
    "x0": ((0, 0, 0), 0, (1, 0, 0)),
    "x1": ((0, 0, 0), 1, (1, 0, 0)),
    "p0": ((0, 0, 0), 0, (0, 1, 0)),
    "p1": ((0, 0, 0), 1, (0, 1, 0)),
    "m0": ((0, 0, 0), 0, (0, -1, 0)),
    "m1": ((0, 0, 0), 1, (0, -1, 0)),
    "pp": ((0, -1, 0), 0, (0, 1, 0)),
    "mm": ((0, 1, 0), 1, (0, -1, 0)),
    "xp0": ((1, 0, 0), 0, (0, 1, 0)),
    "xp1": ((1, 0, 0), 1, (0, 1, 0)),
    "xm0": ((1, 0, 0), 0, (0, -1, 0)),
    "xm1": ((1, 0, 0), 1, (0, -1, 0)),
    "xpp": ((1, -1, 0), 0, (0, 1, 0)),
    "xmm": ((1, 1, 0), 1, (0, -1, 0)),
    "c": ((0, 0, 0), None, (0, 0, 1)),
    "cp": ((0, -1, 0), None, (0, 0, 1)),
    "cm": ((0, 1, 0), None, (0, 0, 1)),
    "cq0": ((0, 2, 0), 0, (0, 0, 1)),
    "cq1": ((0, 2, 0), 1, (0, 0, 1)),
    "cx": ((1, 0, 0), None, (0, 0, 1)),
    "cxp": ((1, -1, 0), None, (0, 0, 1)),
    "cxm": ((1, 1, 0), None, (0, 0, 1)),
    "cxq0": ((1, 2, 0), 0, (0, 0, 1)),
    "cxq1": ((1, 2, 0), 1, (0, 0, 1)),
}
INT_STEPS = {
    "x": ((0, 0), None, (1, 0)),
    "p": ((0, 0), None, (0, 1)),
    "m": ((0, 0), None, (0, -1)),
    "pp": ((0, -1), 0, (0, 1)),
    "mm": ((0, 1), 1, (0, -1)),
    "xp": ((1, 0), None, (0, 1)),
    "xm": ((1, 0), None, (0, -1)),
    "xpp": ((1, -1), 0, (0, 1)),
    "xmm": ((1, 1), 1, (0, -1)),
}


def ladder_kernel(
    int_tiles, amp_mask, pair_dest, amp_hbm, int_hbm, out,
    amp_in, int_in, table_in, table, panel, comp, dense, select, key, acc, lad, stage,
    load_sem, table_sem, amp_send, amp_recv, int_send, int_recv, out_send, out_recv, own_sem,
):
    row, col = lax.axis_index("row"), lax.axis_index("col")
    n_cols = lax.axis_size("col")
    n_rows = lax.axis_size("row")
    pair_rows, amp_cols = amp_hbm.shape
    k_tiles, _, int_cols = int_hbm.shape
    n_tiles = int_cols // TILE
    n_chunks = n_tiles // CHUNK_TILES
    half_rows = pair_rows // 2

    core, y, x_hi = lax.rem(col, 2), lax.rem(lax.div(col, 2), 4), lax.div(col, 8)
    z, x_lo = lax.rem(row, 4), lax.div(row, 4)

    def col_at(dx, dy, dc):
        return lax.rem(x_hi + dx + 2, 2) * 8 + lax.rem(y + dy + 4, 4) * 2 + lax.rem(core + dc + 2, 2)

    def row_at(dx, dz):
        return lax.rem(x_lo + dx + 2, 2) * 4 + lax.rem(z + dz + 4, 4)

    load_amp = pltpu.make_async_copy(amp_hbm, amp_in, load_sem.at[0])
    load_amp.start()
    load_ints = [
        pltpu.make_async_copy(
            int_hbm.at[:, :, n * TILE:(n + 1) * TILE], int_in.at[n * k_tiles:(n + 1) * k_tiles], load_sem.at[1 + n]
        )
        for n in range(n_tiles)
    ]
    for load in load_ints:
        load.start()

    barrier = pltpu.get_barrier_semaphore()
    for step in range(1, n_cols):
        peer = lax.rem(col + step, n_cols)
        pl.semaphore_signal(barrier, inc=1, device_id=(row, peer), device_id_type=MESH)
    for dx, dz in ((1, 0), (0, 1), (0, -1)):
        pl.semaphore_signal(barrier, inc=1, device_id=(row_at(dx, dz), col), device_id_type=MESH)

    block_tiles = k_tiles * n_tiles
    slots = int_tiles.shape[1]
    lane = lax.broadcasted_iota(jnp.int32, (n_rows, TILE), 1)
    owner_row = lax.broadcasted_iota(jnp.int32, (n_rows, TILE), 0)
    tile_of = jnp.where(lane < block_tiles, lax.rem(lane, k_tiles) * n_tiles + lax.div(lane, k_tiles), -1)
    present = jnp.zeros((n_rows, TILE), jnp.int32)
    for r in range(n_rows):
        for s in range(slots):
            present = jnp.where((owner_row == r) & (tile_of == int_tiles[r, s]), 1, present)
    before_lane = lax.broadcasted_iota(jnp.int32, (TILE, TILE), 0) < lax.broadcasted_iota(jnp.int32, (TILE, TILE), 1)
    rank = jnp.dot(
        present.astype(jnp.float32).astype(jnp.bfloat16),
        jnp.where(before_lane, 1.0, 0.0).astype(jnp.bfloat16),
        preferred_element_type=jnp.float32,
    ).astype(jnp.int32)
    first = 0
    for g, count in enumerate(GROUPS):
        inside = (present == 1) & (rank >= first) & (rank < first + count)
        place = jnp.where(inside, owner_row * count + rank - first, n_rows * count)
        table_in[g * n_rows:(g + 1) * n_rows, :] = jnp.clip(place, 0, n_rows * count)
        first += count
    own_place = jnp.sum(
        jnp.where((owner_row == row) & (present == 1), rank + 1, 0).astype(jnp.float32), axis=0, keepdims=True
    )
    slot_at = lax.broadcasted_iota(jnp.int32, (slots, TILE), 0).astype(jnp.float32) + 1.0
    tile_at = lax.broadcasted_iota(jnp.int32, (slots, TILE), 1).astype(jnp.float32)
    own_tile = jnp.sum(jnp.where(own_place == slot_at, tile_at, 0.0), axis=1, keepdims=True)
    own_first = len(GROUPS) * n_rows
    table_in[own_first:own_first + slots, :] = jnp.clip(
        jnp.broadcast_to(own_tile, (slots, TILE)).astype(jnp.int32), 0, block_tiles - 1
    )
    load_table = pltpu.make_async_copy(table_in, table, table_sem)
    load_table.start()

    def amp_copy(name, seen_by_receiver):
        what, half, to = AMP_STEPS[name]
        sem = list(AMP_STEPS).index(name)
        owner = col_at(*(w - t for w, t in zip(what, to))) if seen_by_receiver else col_at(*what)
        at = pl.ds(pl.multiple_of(owner * amp_cols, amp_cols), amp_cols)
        piece = panel.at[:, at] if half is None else panel.at[half * half_rows:(half + 1) * half_rows, at]
        return pltpu.make_async_remote_copy(
            piece, piece, amp_send.at[sem], amp_recv.at[sem], device_id=(row, col_at(*to)), device_id_type=MESH
        )

    def int_copy(g, name, seen_by_receiver):
        what, half, to = INT_STEPS[name]
        sem = list(INT_STEPS).index(name)
        owner = row_at(*(w - t for w, t in zip(what, to))) if seen_by_receiver else row_at(*what)
        count = GROUPS[g]
        if half is None:
            piece = comp[g].at[pl.ds(owner * count, count)]
        else:
            piece = comp[g].at[pl.ds(owner * count + half * (count // 2), count // 2)]
        return pltpu.make_async_remote_copy(
            piece, piece, int_send.at[g, sem], int_recv.at[g, sem], device_id=(row_at(*to), col), device_id_type=MESH
        )

    def amp_start(*names):
        for name in names:
            amp_copy(name, False).start()

    def amp_arrived(*names):
        for name in names:
            amp_copy(name, True).wait_recv()

    def int_start(g, *names):
        for name in names:
            int_copy(g, name, False).start()

    def int_arrived(g, *names):
        for name in names:
            int_copy(g, name, True).wait_recv()

    load_amp.wait()
    own_cols = pl.multiple_of(col * amp_cols, amp_cols)
    kept = amp_mask[...].astype(jnp.float32).astype(jnp.bfloat16)
    for a in range(pair_rows // TILE):
        for k in range(amp_cols // TILE):
            tile = amp_in[a * TILE:(a + 1) * TILE, k * TILE:(k + 1) * TILE]
            panel[a * TILE:(a + 1) * TILE, pl.ds(own_cols + k * TILE, TILE)] = tile * kept[k:k + 1, a:a + 1]
    pl.semaphore_wait(barrier, n_cols - 1 + 3)
    amp_start("x0", "p0", "m1", "x1", "p1", "m0", "c")

    load_table.wait()
    for load in load_ints:
        load.wait()
    first = 0
    for g, count in enumerate(GROUPS):
        for slot in range(count):
            comp[g][row * count + slot] = int_in[table[own_first + first + slot, 0]]
        comp[g][n_rows * count] = jnp.zeros((TILE, TILE), jnp.bfloat16)
        first += count
    int_start(0, "x", "p", "m")
    int_start(1, "p", "m")

    dest_all = lax.broadcasted_iota(jnp.int32, (n_cols, pair_rows), 0)
    onehot = jnp.where(dest_all == pair_dest[...], 1.0, 0.0)
    for block in range(pair_rows // TILE):
        cols = slice(block * TILE, (block + 1) * TILE)
        q = lax.broadcasted_iota(jnp.int32, (pair_rows, TILE), 0)
        p = lax.broadcasted_iota(jnp.int32, (pair_rows, TILE), 1) + block * TILE
        earlier = jnp.where(q < p, 1.0, 0.0).astype(jnp.bfloat16)
        before = jnp.dot(onehot.astype(jnp.bfloat16), earlier, preferred_element_type=jnp.float32)
        slot = jnp.sum(before * onehot[:, cols], axis=0, keepdims=True)
        ahead = pair_dest[:, cols] - col - FIRST_STEP + n_cols
        ahead = jnp.where(ahead < 0, ahead + n_cols, ahead)
        key[:, cols] = jnp.where(ahead >= n_cols, ahead - n_cols, ahead) * CAP + slot.astype(jnp.int32)

    def fill_select(d, carry):
        places = lax.broadcasted_iota(jnp.int32, (CAP, pair_rows), 0) + d * CAP
        at = pl.ds(pl.multiple_of(d * CAP, CAP), CAP)
        select[at, :] = jnp.where(places == key[...], 1.0, 0.0).astype(jnp.bfloat16)
        return carry

    lax.fori_loop(0, n_cols, fill_select, 0)

    def unpack(q, groups):
        def one_row(r, carry):
            for n in range(CHUNK_TILES):
                for k in range(k_tiles):
                    tile = None
                    for g in range(groups):
                        at = table[g * n_rows + r, (q * CHUNK_TILES + n) * k_tiles + k]
                        part = comp[g][at]
                        tile = part if tile is None else tile + part
                    down = pl.ds(pl.multiple_of((r * k_tiles + k) * TILE, TILE), TILE)
                    dense[down, n * TILE:(n + 1) * TILE] = tile
            return carry

        lax.fori_loop(0, n_rows, one_row, 0)

    def multiply(start, depth, first, last):
        m_rows = pair_rows // 2

        def one_half(m, carry):
            at = pl.ds(pl.multiple_of(m * m_rows, m_rows), m_rows)
            deep = pl.ds(pl.multiple_of(start, 512), depth)
            total = jnp.dot(panel[at, deep], dense[deep, :], preferred_element_type=jnp.float32)
            if not first:
                total = total + acc[at, :]
            if last:
                lad[at, :] = total.astype(jnp.bfloat16)
            else:
                acc[at, :] = total
            return carry

        lax.fori_loop(0, 2, one_half, 0)

    def out_piece(owner, q):
        return out.at[:, pl.ds(pl.multiple_of(owner * int_cols + q * CHUNK, CHUNK), CHUNK)]

    n_parts = n_cols // PART
    own_place_at = n_cols - FIRST_STEP

    def send_part(q, j):
        for place in range(j * PART, (j + 1) * PART):
            step = (place + FIRST_STEP) % n_cols
            peer = lax.rem(col + step, n_cols)

            def to_peer():
                pltpu.make_async_remote_copy(
                    stage.at[q, place], out_piece(col, q), out_send.at[step], out_recv.at[step],
                    device_id=(row, peer), device_id_type=MESH,
                ).start()

            if step == 0:
                pltpu.make_async_copy(stage.at[q, own_place_at], out_piece(col, q), own_sem.at[q]).start()
            else:
                to_peer()


    def spread(q):
        for j in range(n_parts):
            at = slice(j * PART * CAP, (j + 1) * PART * CAP)
            rows = jnp.dot(select[at, :], lad[...], preferred_element_type=jnp.float32).astype(jnp.bfloat16)
            stage[q, j * PART:(j + 1) * PART] = rows.reshape(PART, CAP, CHUNK)
            if j > 0:
                send_part(q, j - 1)

    def chunks(lo, hi, groups):
        def one_chunk(q, carry):
            unpack(q, groups)
            send_part(q - 1, n_parts - 1)
            multiply(0, n_cols * amp_cols, True, True)
            spread(q)
            return carry

        lax.fori_loop(lo, hi, one_chunk, 0)

    amp_arrived("p0", "m1")
    amp_start("pp", "mm")
    int_arrived(0, "p", "m")
    int_start(0, "pp", "mm")
    amp_arrived("x0", "x1")
    amp_start("xp0", "xm1", "xp1", "xm0", "cx")
    int_start(1, "x")
    amp_arrived("p1", "m0")
    amp_start("cp", "cm")
    int_arrived(1, "p", "m")
    int_start(1, "pp", "mm")
    amp_arrived("pp", "mm")
    amp_start("cq0", "cq1")
    int_arrived(0, "x")
    int_start(0, "xp", "xm")
    int_start(2, "x")
    amp_arrived("xp0", "xm1")
    amp_start("xpp", "xmm")
    int_arrived(0, "xp", "xm")
    int_start(0, "xpp", "xmm")
    int_start(3, "x")
    int_arrived(1, "x")
    int_start(1, "xp", "xm")
    int_start(2, "p", "m")
    amp_arrived("c", "cp", "cm", "cq0", "cq1")
    amp_arrived("xp1", "xm0")
    amp_start("cxp", "cxm")
    int_arrived(0, "pp", "mm", "xpp", "xmm")

    y_cols = 2 * amp_cols
    x_cols = 4 * y_cols
    far = lax.rem(x_hi + 1, 2) * x_cols
    unpack(0, 1)
    multiply(x_hi * x_cols, x_cols, True, False)
    amp_arrived("cx")
    multiply(far + y * y_cols, y_cols, False, False)
    amp_arrived("xpp")
    amp_start("cxq0")
    amp_arrived("xmm")
    amp_start("cxq1")
    int_arrived(1, "xp", "xm")
    int_start(1, "xpp", "xmm")
    int_arrived(2, "x")
    int_start(2, "xp", "xm")
    amp_arrived("cxp")
    multiply(far + lax.rem(y + 3, 4) * y_cols, y_cols, False, False)
    amp_arrived("cxm")
    multiply(far + lax.rem(y + 1, 4) * y_cols, y_cols, False, False)
    amp_arrived("cxq0", "cxq1")
    multiply(far + lax.rem(y + 2, 4) * y_cols, y_cols, False, True)
    spread(0)

    int_arrived(2, "p", "m")
    int_start(2, "pp", "mm")
    int_start(3, "p", "m")
    int_arrived(1, "pp", "mm", "xpp", "xmm")
    chunks(1, 2, 2)
    int_arrived(2, "xp", "xm")
    int_start(2, "xpp", "xmm")
    int_arrived(3, "x")
    int_start(3, "xp", "xm")
    int_arrived(3, "p", "m")
    int_start(3, "pp", "mm")
    int_arrived(2, "pp", "mm", "xpp", "xmm")
    chunks(2, 3, 3)
    int_arrived(3, "xp", "xm")
    int_start(3, "xpp", "xmm")
    int_arrived(3, "pp", "mm", "xpp", "xmm")
    chunks(3, n_chunks, 4)

    for name in AMP_STEPS:
        amp_copy(name, False).wait_send()
    send_part(n_chunks - 1, n_parts - 1)
    for g in range(len(GROUPS)):
        for name in INT_STEPS:
            int_copy(g, name, False).wait_send()

    def own_done(q, carry):
        pltpu.make_async_copy(stage.at[q, own_place_at], out_piece(col, q), own_sem.at[q]).wait()
        return carry

    lax.fori_loop(0, n_chunks, own_done, 0)

    def peer_done(step, carry):
        source = lax.rem(col - step + n_cols, n_cols)
        block = out.at[:, pl.ds(pl.multiple_of(source * int_cols, int_cols), int_cols)]
        whole = pltpu.make_async_remote_copy(
            block, block, out_send.at[step], out_recv.at[step], device_id=(row, source), device_id_type=MESH
        )
        whole.wait()
        return carry

    lax.fori_loop(1, n_cols, peer_done, 0)


def copy_kernel(src, dst, sem):
    rows = TILE // sem.shape[0]
    writes = [
        pltpu.make_async_copy(src.at[i * rows:(i + 1) * rows], dst.at[i * rows:(i + 1) * rows], sem.at[i])
        for i in range(sem.shape[0])
    ]
    for write in writes:
        write.start()
    for write in writes:
        write.wait()


def on_device(amplitudes, amp_mask, integrals, int_tiles, pair_dest):
    pair_rows, amp_cols = amplitudes.shape
    int_rows, int_cols = integrals.shape
    n_rows, n_cols = lax.axis_size("row"), lax.axis_size("col")
    k_tiles, n_tiles = int_rows // TILE, int_cols // TILE
    block_tiles = k_tiles * n_tiles
    slots = int_tiles.shape[2]
    n_chunks = n_tiles // CHUNK_TILES

    any_ref = pl.BlockSpec(memory_space=pl.ANY)
    hbm = pl.BlockSpec(memory_space=pltpu.HBM)
    smem = pl.BlockSpec(memory_space=pltpu.SMEM)
    vmem = pl.BlockSpec(memory_space=pltpu.VMEM)
    spread = pl.pallas_call(
        ladder_kernel,
        out_shape=pltpu.VMEM((CAP, n_cols * int_cols), jnp.bfloat16),
        in_specs=[smem, vmem, vmem, hbm, hbm],
        out_specs=vmem,
        scratch_shapes=[
            pltpu.VMEM((pair_rows, amp_cols), jnp.bfloat16),
            pltpu.VMEM((block_tiles, TILE, TILE), jnp.bfloat16),
            pltpu.VMEM((len(GROUPS) * n_rows + slots, TILE), jnp.int32),
            pltpu.SMEM((len(GROUPS) * n_rows + slots, TILE), jnp.int32),
            pltpu.VMEM((pair_rows, n_cols * amp_cols), jnp.bfloat16),
            [pltpu.VMEM((n_rows * count + 1, TILE, TILE), jnp.bfloat16) for count in GROUPS],
            pltpu.VMEM((n_rows * int_rows, CHUNK), jnp.bfloat16),
            pltpu.VMEM((n_cols * CAP, pair_rows), jnp.bfloat16),
            pltpu.VMEM((1, pair_rows), jnp.int32),
            pltpu.VMEM((pair_rows, CHUNK), jnp.float32),
            pltpu.VMEM((pair_rows, CHUNK), jnp.bfloat16),
            pltpu.VMEM((n_chunks, n_cols, CAP, CHUNK), jnp.bfloat16),
            pltpu.SemaphoreType.DMA((1 + n_tiles,)),
            pltpu.SemaphoreType.DMA,
            pltpu.SemaphoreType.DMA((len(AMP_STEPS),)),
            pltpu.SemaphoreType.DMA((len(AMP_STEPS),)),
            pltpu.SemaphoreType.DMA((len(GROUPS), len(INT_STEPS))),
            pltpu.SemaphoreType.DMA((len(GROUPS), len(INT_STEPS))),
            pltpu.SemaphoreType.DMA((n_cols,)),
            pltpu.SemaphoreType.DMA((n_cols,)),
            pltpu.SemaphoreType.DMA((n_chunks,)),
        ],
        name="ladder",
        compiler_params=pltpu.CompilerParams(
            collective_id=0, has_side_effects=True, vmem_limit_bytes=111 * 512 * 1024
        ),
    )(
        int_tiles.reshape(n_rows, slots), amp_mask.T, pair_dest.reshape(1, pair_rows), amplitudes,
        integrals.reshape(k_tiles, TILE, int_cols),
    )
    return pl.pallas_call(
        copy_kernel,
        out_shape=jax.ShapeDtypeStruct(spread.shape, spread.dtype),
        in_specs=[vmem],
        out_specs=any_ref,
        scratch_shapes=[pltpu.SemaphoreType.DMA((4,))],
        name="deliver",
        compiler_params=pltpu.CompilerParams(vmem_limit_bytes=4 * 1024 * 1024),
    )(spread)


def solution(mesh):
    in_specs = (P("row", "col"), P("row", "col"), P("row", "col"), P(None, "col", None), P("row"))
    out_specs = P(("row", "col"), None)
    return jax.shard_map(
        on_device, mesh=mesh, in_specs=in_specs, out_specs=out_specs, check_vma=False
    )
```
